32 devices in a mesh: groups: 2 (over x), ctx: 16 (over z, y, core).
Axes of the slice: x: 2, y: 2, z: 4, core: 2. Of those that a mesh axis runs over, the one named last changes fastest.
Arguments:
- value_stream: bfloat16 [4096, 2048], P(('groups', 'ctx')), parts along dimension 0, may hold values from -6 to 6
- gate_stream: bfloat16 [4096, 2048], P(('groups', 'ctx')), parts along dimension 0, may hold values from -6 to 6
- filter_spectrum: bfloat16 [2, 2, 2048, 2048], P(None, None, 'ctx'), may hold values from -6 to 6
- router: bfloat16 [2048, 16], replicated, may hold values from -0.125 to 0.125
- w_gate: bfloat16 [2048, 45056], P(None, 'ctx'), may hold values from -0.125 to 0.125
- w_up: bfloat16 [2048, 45056], P(None, 'ctx'), may hold values from -0.125 to 0.125
- w_down: bfloat16 [45056, 2048], P('ctx'), may hold values from -0.109375 to 0.109375
- route_ids: int32 [2, 4096], P(None, ('groups', 'ctx')), parts along dimension 1, may hold values from 0 to 15, as said below
- route_slots: int32 [2, 4096], P(None, ('groups', 'ctx')), parts along dimension 1, may hold values from 0 to 20, as said below
Outputs:
- layer_out: bfloat16 [4096, 2048], P(('groups', 'ctx')), parts along dimension 0
The draws below stay inside these ranges and needn't reach their ends.
There are 2 independent parts, one for each index of `groups`. The reference program is written for one: setup_inputs(seed, part) draws one part's arguments, and reference() takes and returns one part's arrays. A program takes and returns all parts, laid end to end along the dimension named above; an argument that names none is the same for every part. Nothing has to cross between parts.
Inputs may be any that keep to these rules, and one draw needn't show every extreme that they name: `route_ids`: each token names 2 different experts. route_slots[k, r] is the number of earlier choices of the same expert among the tokens of r's ctx index, tokens taken in order and a token's choices in order k = 0, 1, clipped to 20; so at most 20 choices of one expert from one ctx index are kept, and in every draw some expert has its 20 slots filled from every ctx index.
All inputs are finite; a program needn't handle non-finite values.
Results may differ from the reference program's by a relative error of at most 0.0058.
Values may be sent and summed in bfloat16 or wider, within the bound.
A program may use at most 128 MiB of HBM per device.

```python
import jax
import jax.numpy as jnp
import numpy as np
from jax import lax

D = 2048
FF = 2816
EXPERTS = 16
TOP = 2
TOK_DEV = 128
LENGTH = 2048
CAP = 20
N_CTX = 16


def permute_rows(key_one):
    return jax.random.permutation(key_one, TOK_DEV)


def route_table(key):
    rows_total = TOK_DEV * N_CTX
    key_base, key_popular, key_hot, key_perm = jax.random.split(key, 4)
    base_score = jax.random.randint(key_base, (rows_total, EXPERTS), 0, 64)
    popular = jax.random.randint(key_popular, (EXPERTS,), 0, 48)
    hot_expert = jax.random.randint(key_hot, (), 0, EXPERTS)
    row_ranks = jax.vmap(permute_rows)(jax.random.split(key_perm, N_CTX)).reshape(rows_total)
    expert_range = jnp.arange(EXPERTS, dtype=jnp.int32)
    hot_mask = (row_ranks < 2 * CAP)[:, None] & (expert_range[None, :] == hot_expert)
    scores = (base_score + popular[None, :] + 1000 * hot_mask.astype(jnp.int32)) * EXPERTS + expert_range[None, :]
    top_scores, chosen = lax.top_k(scores, TOP)
    chosen = chosen.astype(jnp.int32)
    onehot = (chosen[:, :, None] == expert_range[None, None, :]).astype(jnp.int32).reshape(N_CTX, TOK_DEV * TOP, EXPERTS)
    running = jnp.cumsum(onehot, axis=1) - onehot
    slot_rank = jnp.sum(running * onehot, axis=2).reshape(rows_total, TOP)
    slot_rank = jnp.minimum(slot_rank, CAP)
    return (chosen.T, slot_rank.T)


def draw_route_ids(key, part):
    return route_table(jax.random.fold_in(key, 11))[0].astype(jnp.int32)


def draw_route_slots(key, part):
    return route_table(jax.random.fold_in(key, 11))[1].astype(jnp.int32)


def shard_levels(rng, extent, pieces, low, largest):
    factor_of, own = 1.0, jax.random.fold_in(rng, 6)
    for dim, parts in pieces:
        draws = jnp.exp(jax.random.uniform(jax.random.fold_in(own, dim), (parts,), jnp.float32, low / len(pieces), largest / len(pieces)))
        factor_of = factor_of * jnp.repeat(draws, extent[dim] // parts).reshape([-1 if axis == dim else 1 for axis in range(len(extent))])
    return factor_of


def normal_values(own_key, extent, width, bound, pieces=(), held_as=jnp.bfloat16):
    gain = shard_levels(own_key, extent, pieces, -0.22, 0.18) if pieces else 1.0
    result = jax.random.normal(own_key, extent, jnp.float32) * width * gain
    return jnp.minimum(jnp.maximum(result, -bound), bound).astype(held_as)


def setup_inputs(seed: int = 0, part: int = 0) -> dict:
    key_of = jax.random.split(jax.random.key(seed), 10)
    part_splits = jax.random.split(jax.random.fold_in(key_of[9], part), 10)
    return {
        "value_stream": normal_values(part_splits[0], (LENGTH, D), 1.0, 6.0, ((0, 16),)),
        "gate_stream": normal_values(part_splits[1], (LENGTH, D), 1.0, 6.0, ((0, 16),)),
        "filter_spectrum": normal_values(key_of[2], (2, 2, LENGTH, D), 1.0, 6.0, ((2, 16),)),
        "router": normal_values(key_of[3], (D, EXPERTS), D ** -0.5, 0.125),
        "w_gate": normal_values(key_of[4], (D, EXPERTS * FF), D ** -0.5, 0.125, ((1, 16),)),
        "w_up": normal_values(key_of[5], (D, EXPERTS * FF), D ** -0.5, 0.125, ((1, 16),)),
        "w_down": normal_values(key_of[6], (EXPERTS * FF, D), FF ** -0.5, 0.109375, ((0, 16),)),
        "route_ids": draw_route_ids(jax.random.fold_in(jax.random.fold_in(key_of[9], part), 71), part),
        "route_slots": draw_route_slots(jax.random.fold_in(jax.random.fold_in(key_of[9], part), 71), part),
    }


def reverse_bits(length_n):
    bit_count = length_n.bit_length() - 1
    positions = np.arange(length_n)
    reversed_index = np.zeros(length_n, dtype=np.int64)
    for position in range(bit_count):
        reversed_index = reversed_index | (positions >> position & 1) << bit_count - 1 - position
    return reversed_index

def reference(value_stream, gate_stream, filter_spectrum, router, w_gate, w_up, w_down, route_ids, route_slots):
    bit_order = reverse_bits(LENGTH)
    natural = np.arange(2 * LENGTH)
    parity = natural % 2
    index_n = bit_order[natural // 2]
    filter_real = filter_spectrum[0][parity, index_n].astype(jnp.float32)
    filter_imag = filter_spectrum[1][parity, index_n].astype(jnp.float32)
    inputs = value_stream.astype(jnp.float32)
    padded = jnp.concatenate([inputs, jnp.zeros_like(inputs)], axis=0)
    spectrum = jnp.fft.fft(padded, axis=0)
    product = spectrum * (filter_real + 1j * filter_imag)
    long_conv = jnp.real(jnp.fft.ifft(product, axis=0))[:LENGTH]
    hyena_out = (gate_stream.astype(jnp.float32) * long_conv).astype(jnp.bfloat16)
    hyena32 = hyena_out.astype(jnp.float32)
    inv_rms = lax.rsqrt(lax.optimization_barrier(jnp.mean(hyena32 * hyena32, axis=1, keepdims=True)) + 1e-06)
    normed = (hyena32 * inv_rms).astype(jnp.bfloat16)
    logits = jnp.dot(normed, router, preferred_element_type=jnp.float32)
    device_of = (jnp.arange(LENGTH) // TOK_DEV).astype(jnp.int32)
    slot_total = N_CTX * EXPERTS * CAP
    buffer = jnp.zeros((slot_total + 1, D), jnp.bfloat16)
    for pick_index in range(TOP):
        expert_ids = route_ids[pick_index].astype(jnp.int32)
        slot_ids = route_slots[pick_index].astype(jnp.int32)
        target = jnp.where(slot_ids < CAP, (device_of * EXPERTS + expert_ids) * CAP + slot_ids, slot_total).astype(jnp.int32)
        buffer = buffer.at[target].set(normed)
    buffer = buffer[:slot_total].reshape(N_CTX, EXPERTS, CAP, D)
    owner_split = N_CTX // EXPERTS
    group_size = FF // owner_split
    gate_stack = w_gate.reshape(D, EXPERTS, FF).transpose(1, 0, 2)
    up_stack = w_up.reshape(D, EXPERTS, FF).transpose(1, 0, 2)
    down_stack = w_down.reshape(EXPERTS, FF, D)

    def one_expert(operands):
        slot_rows, gate_weight, up_weight, down_weight = operands
        flat_rows = slot_rows.reshape(N_CTX * CAP, D)
        gate_part = jnp.dot(flat_rows, gate_weight, preferred_element_type=jnp.float32)
        up_part = jnp.dot(flat_rows, up_weight, preferred_element_type=jnp.float32)
        hidden = (jax.nn.silu(gate_part) * up_part).astype(jnp.bfloat16)
        partial_value = jnp.einsum('rsf,sfd->srd', hidden.reshape(N_CTX * CAP, owner_split, group_size).astype(jnp.float32), down_weight.reshape(owner_split, group_size, D).astype(jnp.float32), precision=lax.Precision.HIGHEST).astype(jnp.bfloat16)
        return lax.optimization_barrier(jnp.sum(partial_value.astype(jnp.float32), axis=0))
    expert_out = lax.map(one_expert, (buffer.transpose(1, 0, 2, 3), gate_stack, up_stack, down_stack))
    expert_out = expert_out.reshape(EXPERTS, N_CTX, CAP, D)
    total_sum = hyena32
    for pick_index in range(TOP):
        expert_ids = route_ids[pick_index].astype(jnp.int32)
        slot_ids = route_slots[pick_index].astype(jnp.int32)
        kept_mask = slot_ids < CAP
        safe_slot = jnp.minimum(slot_ids, CAP - 1).astype(jnp.int32)
        picked = expert_out[expert_ids, device_of, safe_slot]
        gate_value = jax.nn.sigmoid(jnp.take_along_axis(logits, expert_ids[:, None], axis=1)[:, 0])
        total_sum = total_sum + jnp.where(kept_mask[:, None], gate_value[:, None] * picked, 0.0)
    return total_sum.astype(jnp.bfloat16)
```

```python
import jax
import jax.numpy as jnp
import numpy as np
from jax import lax
from jax.sharding import PartitionSpec as P

CAP = 20


two_pi = 2.0 * np.pi
highest = lax.Precision.HIGHEST


def reverse_bits(length_n):
    bit_count = length_n.bit_length() - 1
    positions = np.arange(length_n)
    reversed_index = np.zeros(length_n, dtype=np.int64)
    for position in range(bit_count):
        reversed_index = reversed_index | (positions >> position & 1) << bit_count - 1 - position
    return reversed_index


def spread_table(size_ctx):
    rho = 2 * reverse_bits(size_ctx)[None, :] + np.arange(2)[:, None]
    angle_rad = -two_pi * (np.outer(rho.reshape(-1), np.arange(size_ctx)) % (2 * size_ctx)) / (2 * size_ctx)
    parts = np.stack([np.cos(angle_rad), np.sin(angle_rad)], axis=1)
    return jnp.asarray(parts, jnp.float32)


def fine_table(size_ctx, tok_rows):
    total = 2 * size_ctx * tok_rows
    rho = (2 * reverse_bits(size_ctx)[None, :] + np.arange(2)[:, None]).reshape(-1)
    k = 2 * size_ctx * reverse_bits(tok_rows)[None, :] + rho[:, None]
    step = (k[:, :, None] * np.arange(tok_rows)[None, None, :]) % total
    angle_rad = -two_pi * step / total
    re, im = np.cos(angle_rad), np.sin(angle_rad)
    table = np.stack([np.stack([re, -im], axis=2), np.stack([im, re], axis=2)], axis=1)
    return jnp.asarray(table.reshape(2 * size_ctx, 2 * tok_rows, 2 * tok_rows), jnp.float32)


def convolve(arrived, filter_all, size_ctx, tok_rows, block):
    rho_count = 2 * size_ctx
    coarse = spread_table(size_ctx)
    fine = fine_table(size_ctx, tok_rows)
    samples = arrived.astype(jnp.float32).reshape(size_ctx, tok_rows * block)
    spread = jnp.dot(coarse.reshape(2 * rho_count, size_ctx), samples, precision=highest)
    spread = spread.reshape(rho_count, 2 * tok_rows, block)
    signal = jnp.einsum("rqt,rtc->rqc", fine, spread, precision=highest)
    signal = signal.reshape(rho_count, 2, tok_rows, block)
    filter32 = filter_all.astype(jnp.float32).reshape(2, rho_count, tok_rows, block)
    real_part = signal[:, 0] * filter32[0] - signal[:, 1] * filter32[1]
    imag_part = signal[:, 0] * filter32[1] + signal[:, 1] * filter32[0]
    signal = jnp.concatenate([real_part, imag_part], axis=1)
    spread = jnp.einsum("rqt,rqc->rtc", fine, signal, precision=highest)
    spread = spread.reshape(2 * rho_count, tok_rows * block)
    folded = jnp.dot(coarse.reshape(2 * rho_count, size_ctx).T, spread, precision=highest)
    return (folded / (rho_count * tok_rows)).reshape(size_ctx * tok_rows, block)


def local(
    value_stream, gate_stream, filter_spectrum, router, w_gate, w_up, w_down, route_ids, route_slots
):
    tok_rows, channels = value_stream.shape
    size_ctx = lax.axis_size("ctx")
    block = channels // size_ctx
    arrived = lax.all_to_all(value_stream, "ctx", split_axis=1, concat_axis=0, tiled=True)
    filter_all = lax.all_to_all(filter_spectrum, "ctx", split_axis=3, concat_axis=2, tiled=True)
    long_conv = convolve(arrived, filter_all, size_ctx, tok_rows, block)
    long_conv = lax.all_to_all(
        long_conv.astype(jnp.bfloat16), "ctx", split_axis=0, concat_axis=1, tiled=True
    ).astype(jnp.float32)
    hyena_out = (gate_stream.astype(jnp.float32) * long_conv).astype(jnp.bfloat16)
    hyena32 = hyena_out.astype(jnp.float32)
    inv_rms = lax.rsqrt(jnp.mean(hyena32 * hyena32, axis=1, keepdims=True) + 1e-06)
    normed = (hyena32 * inv_rms).astype(jnp.bfloat16)
    logits = jnp.dot(normed, router, preferred_element_type=jnp.float32)
    expert_count = router.shape[1]
    owner_split = size_ctx // expert_count
    slot_count = expert_count * CAP
    positions = jnp.arange(slot_count, dtype=jnp.int32)
    expert_range = jnp.arange(expert_count, dtype=jnp.int32)
    combine = jnp.zeros((tok_rows, slot_count), jnp.float32)
    dispatch = jnp.zeros((slot_count, channels), jnp.float32)
    for pick_index in range(route_ids.shape[0]):
        expert_ids = route_ids[pick_index]
        slot_ids = route_slots[pick_index]
        target = jnp.where(slot_ids < CAP, expert_ids * CAP + slot_ids, -1)
        slot_hits = target[:, None] == positions[None, :]
        chosen_logit = jnp.sum(
            jnp.where(expert_ids[:, None] == expert_range[None, :], logits, 0.0), axis=1
        )
        gate_value = jax.nn.sigmoid(chosen_logit)
        combine = combine + slot_hits.astype(jnp.float32) * gate_value[:, None]
        dispatch = dispatch + lax.dot_general(
            slot_hits.astype(jnp.bfloat16),
            normed,
            (((0,), (0,)), ((), ())),
            preferred_element_type=jnp.float32,
        )
    buffer = dispatch.astype(jnp.bfloat16).reshape(expert_count, CAP, channels)
    outgoing = jnp.repeat(buffer, owner_split, axis=0)
    slot_rows = lax.all_to_all(outgoing, "ctx", split_axis=0, concat_axis=0, tiled=True)
    flat_rows = slot_rows.reshape(-1, channels)
    gate_part = jnp.dot(flat_rows, w_gate, preferred_element_type=jnp.float32)
    up_part = jnp.dot(flat_rows, w_up, preferred_element_type=jnp.float32)
    hidden = (jax.nn.silu(gate_part) * up_part).astype(jnp.bfloat16)
    partial_value = jnp.dot(hidden, w_down, preferred_element_type=jnp.float32).astype(jnp.bfloat16)
    returned = lax.all_to_all(
        partial_value.reshape(slot_rows.shape), "ctx", split_axis=0, concat_axis=0, tiled=True
    )
    expert_out = jnp.sum(
        returned.astype(jnp.float32).reshape(expert_count, owner_split, CAP, channels), axis=1
    ).reshape(slot_count, channels)
    contribution = jnp.dot(combine, expert_out, precision=highest)
    return (hyena32 + contribution).astype(jnp.bfloat16)


def solution(mesh):
    in_specs = (
        P(("groups", "ctx"), None),
        P(("groups", "ctx"), None),
        P(None, None, "ctx", None),
        P(),
        P(None, "ctx"),
        P(None, "ctx"),
        P("ctx", None),
        P(None, ("groups", "ctx")),
        P(None, ("groups", "ctx")),
    )
    out_specs = P(("groups", "ctx"), None)
    return jax.shard_map(local, mesh=mesh, in_specs=in_specs, out_specs=out_specs, check_vma=False)
```

```python
import jax
import jax.numpy as jnp
import numpy as np
from jax import lax
from jax.experimental import pallas as pl
from jax.experimental.pallas import tpu as pltpu
from jax.sharding import PartitionSpec as P

CAP = 20


two_pi = 2.0 * np.pi
highest = lax.Precision.HIGHEST


def reverse_bits(length_n):
    bit_count = length_n.bit_length() - 1
    positions = np.arange(length_n)
    reversed_index = np.zeros(length_n, dtype=np.int64)
    for position in range(bit_count):
        reversed_index = reversed_index | (positions >> position & 1) << bit_count - 1 - position
    return reversed_index


def spread_table(size_ctx):
    rho = 2 * reverse_bits(size_ctx)[None, :] + np.arange(2)[:, None]
    angle_rad = -two_pi * (np.outer(rho.reshape(-1), np.arange(size_ctx)) % (2 * size_ctx)) / (2 * size_ctx)
    parts = np.stack([np.cos(angle_rad), np.sin(angle_rad)], axis=1)
    return jnp.asarray(parts, jnp.float32)


def fine_table(size_ctx, tok_rows):
    total = 2 * size_ctx * tok_rows
    rho = (2 * reverse_bits(size_ctx)[None, :] + np.arange(2)[:, None]).reshape(-1)
    k = 2 * size_ctx * reverse_bits(tok_rows)[None, :] + rho[:, None]
    step = (k[:, :, None] * np.arange(tok_rows)[None, None, :]) % total
    angle_rad = -two_pi * step / total
    re, im = np.cos(angle_rad), np.sin(angle_rad)
    table = np.stack([np.stack([re, -im], axis=2), np.stack([im, re], axis=2)], axis=1)
    return jnp.asarray(table.reshape(2 * size_ctx, 2 * tok_rows, 2 * tok_rows), jnp.float32)


def convolve(arrived, filter_all, size_ctx, tok_rows, block):
    rho_count = 2 * size_ctx
    coarse = spread_table(size_ctx)
    fine = fine_table(size_ctx, tok_rows)
    samples = arrived.astype(jnp.float32).reshape(size_ctx, tok_rows * block)
    spread = jnp.dot(coarse.reshape(2 * rho_count, size_ctx), samples, precision=highest)
    spread = spread.reshape(rho_count, 2 * tok_rows, block)
    signal = jnp.einsum("rqt,rtc->rqc", fine, spread, precision=highest)
    signal = signal.reshape(rho_count, 2, tok_rows, block)
    filter32 = filter_all.astype(jnp.float32).reshape(2, rho_count, tok_rows, block)
    real_part = signal[:, 0] * filter32[0] - signal[:, 1] * filter32[1]
    imag_part = signal[:, 0] * filter32[1] + signal[:, 1] * filter32[0]
    signal = jnp.concatenate([real_part, imag_part], axis=1)
    spread = jnp.einsum("rqt,rqc->rtc", fine, signal, precision=highest)
    spread = spread.reshape(2 * rho_count, tok_rows * block)
    folded = jnp.dot(coarse.reshape(2 * rho_count, size_ctx).T, spread, precision=highest)
    return (folded / (rho_count * tok_rows)).reshape(size_ctx * tok_rows, block)


def flip_bits(index, mask):
    result = index
    bit = 1
    while bit <= mask:
        if mask & bit:
            result = result + bit * (1 - 2 * ((index // bit) % 2))
        bit *= 2
    return result


MASKS = (0, 1, 2, 3, 8, 9, 10, 11, 4, 5, 6, 7, 12, 13, 14, 15)
HEAD = 16
TAIL = CAP - HEAD
QUARTERS = HEAD // TAIL


def expert_kernel(
    conv_ref, stream_ref, router_ref, ids_ref, head_ref, tail_ref, wg_hbm, wu_hbm, wd_hbm, out_ref,
    hyena, send_head, send_tail, recv_head, recv_tail, done_head, done_tail, back_head, back_tail,
    rows, hidden, wg, wu, wd, tail_sum, gates, own_sem, send_sem, recv_sem, weight_sem,
):
    device = lax.axis_index("ctx")
    peers = [flip_bits(device, mask) for mask in MASKS]
    count = len(MASKS)
    channels = conv_ref.shape[1]
    quarter = channels // QUARTERS
    tokens = conv_ref.shape[0]
    slots = count * HEAD
    weights = [
        pltpu.make_async_copy(src, dst, weight_sem.at[i])
        for i, (src, dst) in enumerate(((wg_hbm, wg), (wu_hbm, wu), (wd_hbm, wd)))
    ]
    for copy in weights:
        copy.start()
    barrier = pltpu.get_barrier_semaphore()
    for slot in range(1, count):
        pl.semaphore_signal(
            barrier, inc=1, device_id={"ctx": peers[slot]}, device_id_type=pl.DeviceIdType.MESH
        )
    mixed = (stream_ref[...].astype(jnp.float32) * conv_ref[...].astype(jnp.float32)).astype(jnp.bfloat16)
    hyena[...] = mixed
    mixed32 = mixed.astype(jnp.float32)
    mean = jnp.sum(mixed32 * mixed32, axis=1, keepdims=True) / channels
    normed = (mixed32 * lax.rsqrt(mean + 1e-06)).astype(jnp.bfloat16)
    slot_row = lax.broadcasted_iota(jnp.int32, (slots, tokens), 0)

    def hits(targets, shift):
        return [slot_row == targets[pick : pick + 1, :] + shift for pick in range(2)]

    def one_hot(targets, shift):
        first, second = hits(targets, shift)
        return jnp.where(first | second, 1.0, 0.0).astype(jnp.bfloat16)

    head = head_ref[...]
    tail = tail_ref[...]
    send_head[...] = jnp.dot(one_hot(head, 0), normed, preferred_element_type=jnp.float32).astype(jnp.bfloat16)
    packed = jnp.zeros((slots, quarter), jnp.float32)
    for part in range(QUARTERS):
        packed = packed + jnp.dot(
            one_hot(tail, TAIL * part),
            normed[:, part * quarter : (part + 1) * quarter],
            preferred_element_type=jnp.float32,
        )
    send_tail[...] = packed.astype(jnp.bfloat16)
    pl.semaphore_wait(barrier, count - 1)

    def exchange(slot, phase):
        here = pl.ds(slot * HEAD, HEAD)
        if phase == 0:
            pairs = ((send_head, recv_head), (send_tail, recv_tail))
        else:
            pairs = ((done_head, back_head), (done_tail, back_tail))
        copies = []
        for which, (src, dst) in enumerate(pairs):
            if slot == 0:
                copies.append(pltpu.make_async_copy(src.at[here], dst.at[here], own_sem.at[phase, which]))
            else:
                copies.append(
                    pltpu.make_async_remote_copy(
                        src_ref=src.at[here],
                        dst_ref=dst.at[here],
                        send_sem=send_sem.at[phase, which, slot],
                        recv_sem=recv_sem.at[phase, which, slot],
                        device_id={"ctx": peers[slot]},
                        device_id_type=pl.DeviceIdType.MESH,
                    )
                )
        return copies

    half = count // 2
    issue = (7, 6, 5, 4, 3, 2, 1, 0, 15, 14, 13, 12, 11, 10, 9, 8)
    outward = {slot: exchange(slot, 0) for slot in range(count)}
    inward = {slot: exchange(slot, 1) for slot in range(count)}
    for slot in issue:
        for copy in outward[slot]:
            copy.start()
    logits = lax.dot_general(
        router_ref[...], normed, (((1,), (1,)), ((), ())), preferred_element_type=jnp.float32
    )
    expert_row = lax.broadcasted_iota(jnp.int32, logits.shape, 0)
    ids = ids_ref[...]
    for pick in range(2):
        chosen = jnp.sum(
            jnp.where(expert_row == ids[pick : pick + 1, :], logits, 0.0), axis=0, keepdims=True
        )
        gates[pick : pick + 1, :] = jax.nn.sigmoid(chosen)
    group_rows = half * HEAD
    tail_rows = half * TAIL
    pick_row = lax.broadcasted_iota(jnp.int32, (tail_rows, group_rows), 0)
    pick_col = lax.broadcasted_iota(jnp.int32, (tail_rows, group_rows), 1)
    pick_base = (pick_row // TAIL) * HEAD + pick_row % TAIL
    hidden_size = wg.shape[1]
    for group in range(2):
        for slot in range(group * half, (group + 1) * half):
            for copy in outward[slot]:
                copy.wait()
        span = pl.ds(group * group_rows, group_rows)
        rows[0:group_rows, :] = recv_head[span, :]
        for part in range(QUARTERS):
            select = jnp.where(pick_col == pick_base + TAIL * part, 1.0, 0.0).astype(jnp.bfloat16)
            rows[group_rows : group_rows + tail_rows, part * quarter : (part + 1) * quarter] = jnp.dot(
                select, recv_tail[span, :], preferred_element_type=jnp.float32
            ).astype(jnp.bfloat16)
        if group == 0:
            weights[0].wait()
            weights[1].wait()

        @pl.loop(0, hidden_size // 256)
        def _(step):
            columns = pl.ds(pl.multiple_of(step * 256, 256), 256)
            gate_part = jnp.dot(rows[...], wg[:, columns], preferred_element_type=jnp.float32)
            up_part = jnp.dot(rows[...], wu[:, columns], preferred_element_type=jnp.float32)
            hidden[:, columns] = (jax.nn.silu(gate_part) * up_part).astype(jnp.bfloat16)

        if group == 0:
            weights[2].wait()
        tail_sum[...] = jnp.zeros_like(tail_sum)

        @pl.loop(0, QUARTERS)
        def _(part):
            columns = pl.ds(pl.multiple_of(part * quarter, 256), quarter)
            value = jnp.dot(hidden[...], wd[:, columns], preferred_element_type=jnp.float32).astype(jnp.bfloat16)
            done_head[span, columns] = value[0:group_rows, :]
            select = jnp.where(pick_col == pick_base + TAIL * part, 1.0, 0.0).astype(jnp.bfloat16)
            tail_sum[...] += lax.dot_general(
                select,
                value[group_rows : group_rows + tail_rows, :],
                (((0,), (0,)), ((), ())),
                preferred_element_type=jnp.float32,
            )

        done_tail[span, :] = tail_sum[...].astype(jnp.bfloat16)
        for slot in issue[group * half : (group + 1) * half]:
            for copy in inward[slot]:
                copy.start()

    def weighted(targets, shift, values):
        first, second = hits(targets, shift)
        mix = jnp.where(first, gates[0:1, :], 0.0) + jnp.where(second, gates[1:2, :], 0.0)
        high = mix.astype(jnp.bfloat16)
        low = (mix - high.astype(jnp.float32)).astype(jnp.bfloat16)
        dims = (((0,), (0,)), ((), ()))
        return lax.dot_general(high, values, dims, preferred_element_type=jnp.float32) + lax.dot_general(
            low, values, dims, preferred_element_type=jnp.float32
        )

    for slot in range(count):
        for copy in inward[slot]:
            copy.wait()
    for part in range(QUARTERS):
        columns = slice(part * quarter, (part + 1) * quarter)
        total = hyena[:, columns].astype(jnp.float32)
        total = total + weighted(head, 0, back_head[:, columns])
        total = total + weighted(tail, TAIL * part, back_tail[...])
        out_ref[:, columns] = total.astype(jnp.bfloat16)


def run_experts(long_conv, gate_stream, router, w_gate, w_up, w_down, route_ids, route_slots):
    tokens, channels = gate_stream.shape
    hidden_size = w_gate.shape[1]
    count = len(MASKS)
    slots = count * HEAD
    half_rows = slots // 2 + (count // 2) * TAIL
    quarter = channels // QUARTERS
    device = lax.axis_index("ctx")
    place = jnp.asarray(np.argsort(np.asarray(MASKS)), jnp.int32)
    offset = jnp.bitwise_xor(route_ids, device)
    position = jnp.sum(
        jnp.where(offset[:, :, None] == jnp.arange(count)[None, None, :], place[None, None, :], 0), axis=2
    )
    head = jnp.where(route_slots < HEAD, position * HEAD + route_slots, -1024)
    tail = jnp.where(
        (route_slots >= HEAD) & (route_slots < CAP), position * HEAD + route_slots - HEAD, -1024
    )
    vmem = pl.BlockSpec(memory_space=pltpu.VMEM)
    hbm = pl.BlockSpec(memory_space=pl.ANY)
    bf16 = jnp.bfloat16
    return pl.pallas_call(
        expert_kernel,
        out_shape=jax.ShapeDtypeStruct((tokens, channels), bf16),
        in_specs=[vmem] * 6 + [hbm] * 3,
        out_specs=vmem,
        scratch_shapes=[pltpu.VMEM((tokens, channels), bf16)]
        + [pltpu.VMEM((slots, channels), bf16), pltpu.VMEM((slots, quarter), bf16)] * 4
        + [
            pltpu.VMEM((half_rows, channels), bf16),
            pltpu.VMEM((half_rows, hidden_size), bf16),
            pltpu.VMEM((channels, hidden_size), bf16),
            pltpu.VMEM((channels, hidden_size), bf16),
            pltpu.VMEM((hidden_size, channels), bf16),
            pltpu.VMEM((slots // 2, quarter), jnp.float32),
            pltpu.VMEM((8, tokens), jnp.float32),
            pltpu.SemaphoreType.DMA((2, 2)),
            pltpu.SemaphoreType.DMA((2, 2, count)),
            pltpu.SemaphoreType.DMA((2, 2, count)),
            pltpu.SemaphoreType.DMA((3,)),
        ],
        compiler_params=pltpu.CompilerParams(
            collective_id=1, has_side_effects=True, vmem_limit_bytes=56 * 1024 * 1024
        ),
    )(long_conv, gate_stream, router.T, route_ids, head, tail, w_gate, w_up, w_down)


def local(
    value_stream, gate_stream, filter_spectrum, router, w_gate, w_up, w_down, route_ids, route_slots
):
    tok_rows, channels = value_stream.shape
    size_ctx = lax.axis_size("ctx")
    block = channels // size_ctx
    arrived = lax.all_to_all(value_stream, "ctx", split_axis=1, concat_axis=0, tiled=True)
    filter_all = lax.all_to_all(filter_spectrum, "ctx", split_axis=3, concat_axis=2, tiled=True)
    long_conv = convolve(arrived, filter_all, size_ctx, tok_rows, block)
    long_conv = lax.all_to_all(
        long_conv.astype(jnp.bfloat16), "ctx", split_axis=0, concat_axis=1, tiled=True
    )
    expert_count = router.shape[1]
    if size_ctx == expert_count == len(MASKS) and channels % 512 == 0 and w_gate.shape[1] % 256 == 0:
        return run_experts(
            long_conv, gate_stream, router, w_gate, w_up, w_down, route_ids, route_slots
        )
    long_conv = long_conv.astype(jnp.float32)
    hyena_out = (gate_stream.astype(jnp.float32) * long_conv).astype(jnp.bfloat16)
    hyena32 = hyena_out.astype(jnp.float32)
    inv_rms = lax.rsqrt(jnp.mean(hyena32 * hyena32, axis=1, keepdims=True) + 1e-06)
    normed = (hyena32 * inv_rms).astype(jnp.bfloat16)
    logits = jnp.dot(normed, router, preferred_element_type=jnp.float32)
    owner_split = size_ctx // expert_count
    slot_count = expert_count * CAP
    positions = jnp.arange(slot_count, dtype=jnp.int32)
    expert_range = jnp.arange(expert_count, dtype=jnp.int32)
    combine = jnp.zeros((tok_rows, slot_count), jnp.float32)
    dispatch = jnp.zeros((slot_count, channels), jnp.float32)
    for pick_index in range(route_ids.shape[0]):
        expert_ids = route_ids[pick_index]
        slot_ids = route_slots[pick_index]
        target = jnp.where(slot_ids < CAP, expert_ids * CAP + slot_ids, -1)
        slot_hits = target[:, None] == positions[None, :]
        chosen_logit = jnp.sum(
            jnp.where(expert_ids[:, None] == expert_range[None, :], logits, 0.0), axis=1
        )
        gate_value = jax.nn.sigmoid(chosen_logit)
        combine = combine + slot_hits.astype(jnp.float32) * gate_value[:, None]
        dispatch = dispatch + lax.dot_general(
            slot_hits.astype(jnp.bfloat16),
            normed,
            (((0,), (0,)), ((), ())),
            preferred_element_type=jnp.float32,
        )
    buffer = dispatch.astype(jnp.bfloat16).reshape(expert_count, CAP, channels)
    outgoing = jnp.repeat(buffer, owner_split, axis=0)
    slot_rows = lax.all_to_all(outgoing, "ctx", split_axis=0, concat_axis=0, tiled=True)
    flat_rows = slot_rows.reshape(-1, channels)
    gate_part = jnp.dot(flat_rows, w_gate, preferred_element_type=jnp.float32)
    up_part = jnp.dot(flat_rows, w_up, preferred_element_type=jnp.float32)
    hidden = (jax.nn.silu(gate_part) * up_part).astype(jnp.bfloat16)
    partial_value = jnp.dot(hidden, w_down, preferred_element_type=jnp.float32).astype(jnp.bfloat16)
    returned = lax.all_to_all(
        partial_value.reshape(slot_rows.shape), "ctx", split_axis=0, concat_axis=0, tiled=True
    )
    expert_out = jnp.sum(
        returned.astype(jnp.float32).reshape(expert_count, owner_split, CAP, channels), axis=1
    ).reshape(slot_count, channels)
    contribution = jnp.dot(combine, expert_out, precision=highest)
    return (hyena32 + contribution).astype(jnp.bfloat16)


def solution(mesh):
    in_specs = (
        P(("groups", "ctx"), None),
        P(("groups", "ctx"), None),
        P(None, None, "ctx", None),
        P(),
        P(None, "ctx"),
        P(None, "ctx"),
        P("ctx", None),
        P(None, ("groups", "ctx")),
        P(None, ("groups", "ctx")),
    )
    out_specs = P(("groups", "ctx"), None)
    return jax.shard_map(local, mesh=mesh, in_specs=in_specs, out_specs=out_specs, check_vma=False)
```

```python
import jax
import jax.numpy as jnp
import numpy as np
from jax import lax
from jax.experimental import pallas as pl
from jax.experimental.pallas import tpu as pltpu
from jax.sharding import PartitionSpec as P

CAP = 20


two_pi = 2.0 * np.pi
highest = lax.Precision.HIGHEST


def reverse_bits(length_n):
    bit_count = length_n.bit_length() - 1
    positions = np.arange(length_n)
    reversed_index = np.zeros(length_n, dtype=np.int64)
    for position in range(bit_count):
        reversed_index = reversed_index | (positions >> position & 1) << bit_count - 1 - position
    return reversed_index


def spread_table(size_ctx):
    rho = 2 * reverse_bits(size_ctx)[None, :] + np.arange(2)[:, None]
    angle_rad = -two_pi * (np.outer(rho.reshape(-1), np.arange(size_ctx)) % (2 * size_ctx)) / (2 * size_ctx)
    parts = np.stack([np.cos(angle_rad), np.sin(angle_rad)], axis=1)
    return jnp.asarray(parts, jnp.float32)


def fine_table(size_ctx, tok_rows):
    total = 2 * size_ctx * tok_rows
    rho = (2 * reverse_bits(size_ctx)[None, :] + np.arange(2)[:, None]).reshape(-1)
    k = 2 * size_ctx * reverse_bits(tok_rows)[None, :] + rho[:, None]
    step = (k[:, :, None] * np.arange(tok_rows)[None, None, :]) % total
    angle_rad = -two_pi * step / total
    re, im = np.cos(angle_rad), np.sin(angle_rad)
    table = np.stack([np.stack([re, -im], axis=2), np.stack([im, re], axis=2)], axis=1)
    return jnp.asarray(table.reshape(2 * size_ctx, 2 * tok_rows, 2 * tok_rows), jnp.float32)


def convolve(arrived, filter_all, size_ctx, tok_rows, block):
    rho_count = 2 * size_ctx
    coarse = spread_table(size_ctx)
    fine = fine_table(size_ctx, tok_rows)
    samples = arrived.astype(jnp.float32).reshape(size_ctx, tok_rows * block)
    spread = jnp.dot(coarse.reshape(2 * rho_count, size_ctx), samples, precision=highest)
    spread = spread.reshape(rho_count, 2 * tok_rows, block)
    signal = jnp.einsum("rqt,rtc->rqc", fine, spread, precision=highest)
    signal = signal.reshape(rho_count, 2, tok_rows, block)
    filter32 = filter_all.astype(jnp.float32).reshape(2, rho_count, tok_rows, block)
    real_part = signal[:, 0] * filter32[0] - signal[:, 1] * filter32[1]
    imag_part = signal[:, 0] * filter32[1] + signal[:, 1] * filter32[0]
    signal = jnp.concatenate([real_part, imag_part], axis=1)
    spread = jnp.einsum("rqt,rqc->rtc", fine, signal, precision=highest)
    spread = spread.reshape(2 * rho_count, tok_rows * block)
    folded = jnp.dot(coarse.reshape(2 * rho_count, size_ctx).T, spread, precision=highest)
    return (folded / (rho_count * tok_rows)).reshape(size_ctx * tok_rows, block)


def flip_bits(index, mask):
    result = index
    bit = 1
    while bit <= mask:
        if mask & bit:
            result = result + bit * (1 - 2 * ((index // bit) % 2))
        bit *= 2
    return result


MASKS = (0, 1, 2, 3, 8, 9, 10, 11, 4, 5, 6, 7, 12, 13, 14, 15)
HEAD = 16
TAIL = CAP - HEAD
QUARTERS = HEAD // TAIL


def twist_table(size_ctx, tok_rows):
    rho = (2 * reverse_bits(size_ctx)[:, None] + np.arange(2)[None, :]).reshape(-1)
    angle_rad = -two_pi * np.outer(np.arange(tok_rows), rho) / (2 * size_ctx * tok_rows)
    return jnp.asarray(np.concatenate([np.cos(angle_rad), np.sin(angle_rad)], axis=1), jnp.float32)


def inner_tables(tok_rows):
    angle_rad = -two_pi * (np.outer(reverse_bits(tok_rows), np.arange(tok_rows)) % tok_rows) / tok_rows
    re, im = np.cos(angle_rad), np.sin(angle_rad)
    table = np.block([[re, -im], [im, re]]).astype(np.float32)
    pieces = []
    for matrix in (table, table.T):
        high = matrix.astype(jnp.bfloat16)
        low = (matrix - high.astype(np.float32)).astype(jnp.bfloat16)
        pieces += [high, low]
    return jnp.asarray(np.stack(pieces))


def times_root(pair, power, order):
    power %= order
    re, im = pair
    if power == 0:
        return pair
    if im is None and 4 * power % order:
        cos, sin = float(np.cos(two_pi * power / order)), float(np.sin(two_pi * power / order))
        return (re * cos, re * sin)
    if im is None:
        im = jnp.zeros_like(re)
    if 4 * power == order:
        return (-im, re)
    if 2 * power == order:
        return (-re, -im)
    if 4 * power == 3 * order:
        return (im, -re)
    cos, sin = float(np.cos(two_pi * power / order)), float(np.sin(two_pi * power / order))
    return (re * cos - im * sin, re * sin + im * cos)


def short_transform(values, sign):
    order = len(values)
    if order == 1:
        return values
    even = short_transform(values[0::2], sign)
    odd = short_transform(values[1::2], sign)
    turned = [times_root(odd[i], sign * i, order) for i in range(order // 2)]
    return [(even[i][0] + turned[i][0], even[i][1] + turned[i][1]) for i in range(order // 2)] + [
        (even[i][0] - turned[i][0], even[i][1] - turned[i][1]) for i in range(order // 2)
    ]


def conv_kernel(
    values_ref, filter_ref, tables_ref, twist_ref, out_ref,
    got_values, got_filter, wave_high, wave_low, signal, result,
    own_sem, send_sem, recv_sem, pass_send, pass_recv,
):
    device = lax.axis_index("ctx")
    group = lax.axis_index("groups")
    count = len(MASKS)
    tokens = values_ref.shape[0]
    block = values_ref.shape[1] // count
    peers = [flip_bits(device, mask) for mask in range(count)]
    barrier = pltpu.get_barrier_semaphore()
    for mask in range(1, count):
        pl.semaphore_signal(
            barrier, inc=1, device_id={"ctx": peers[mask]}, device_id_type=pl.DeviceIdType.MESH
        )
    pl.semaphore_signal(
        barrier, inc=1, device_id={"groups": 1 - group}, device_id_type=pl.DeviceIdType.MESH
    )

    def lanes(index):
        return pl.ds(pl.multiple_of(index * block, block), block)

    def to_peer(kind, mask, src, dst):
        return pltpu.make_async_remote_copy(
            src_ref=src,
            dst_ref=dst,
            send_sem=send_sem.at[kind, mask],
            recv_sem=recv_sem.at[kind, mask],
            device_id={"ctx": peers[mask]},
            device_id_type=pl.DeviceIdType.MESH,
        )

    own = [
        pltpu.make_async_copy(values_ref.at[:, lanes(device)], got_values.at[device], own_sem.at[0]),
        pltpu.make_async_copy(
            filter_ref.at[:, :, :, lanes(device)], got_filter.at[:, :, device], own_sem.at[1]
        ),
    ]
    for copy in own:
        copy.start()
    pl.semaphore_wait(barrier, count)
    issue = (15, 14, 13, 12, 11, 10, 9, 8, 7, 6, 5, 4, 3, 2, 1)
    sent_values, sent_filter = {}, {}
    for mask in issue:
        sent_values[mask] = to_peer(
            0, mask, values_ref.at[:, lanes(peers[mask])], got_values.at[device]
        )
        sent_values[mask].start()
    for mask in issue:
        sent_filter[mask] = to_peer(
            1, mask, filter_ref.at[:, group, :, lanes(peers[mask])], got_filter.at[:, group, device]
        )
        sent_filter[mask].start()
    own[0].wait()
    for mask in issue:
        sent_values[mask].wait()

    def reverse(index):
        return int(reverse_bits(count)[index])

    half = tokens
    tile = 16

    @pl.loop(0, tokens // tile)
    def _(step):
        here = pl.ds(pl.multiple_of(step * tile, tile), tile)
        there = pl.ds(pl.multiple_of(half + step * tile, tile), tile)
        samples = [got_values[source, here, :].astype(jnp.float32) for source in range(count)]
        zero = jnp.zeros_like(samples[0])
        for parity in range(2):
            pairs = [
                times_root((item, None), -source * parity, 2 * count)
                for source, item in enumerate(samples)
            ]
            pairs = [(re, zero if im is None else im) for re, im in pairs]
            waves = short_transform(pairs, -1)
            for place in range(count):
                re, im = waves[reverse(place)]
                column = 2 * place + parity
                cos = twist_ref[here, column : column + 1]
                sin = twist_ref[here, 2 * count + column : 2 * count + column + 1]
                for rows, item in ((here, re * cos - im * sin), (there, re * sin + im * cos)):
                    high = item.astype(jnp.bfloat16)
                    columns = slice(column * block, (column + 1) * block)
                    wave_high[rows, columns] = high
                    wave_low[rows, columns] = (item - high.astype(jnp.float32)).astype(jnp.bfloat16)

    width = 4 * block

    def product(which, columns):
        high, low = wave_high[:, columns], wave_low[:, columns]
        return (
            jnp.dot(tables_ref[which], high, preferred_element_type=jnp.float32)
            + jnp.dot(tables_ref[which], low, preferred_element_type=jnp.float32)
            + jnp.dot(tables_ref[which + 1], high, preferred_element_type=jnp.float32)
        )

    steps = 2 * count * block // width

    @pl.loop(0, steps)
    def _(step):
        columns = pl.ds(pl.multiple_of(step * width, width), width)
        signal[:, columns] = product(0, columns)

    own[1].wait()
    passed = {}
    for mask in issue:
        sent_filter[mask].wait()
        slab = got_filter.at[:, group, peers[mask]]
        passed[mask] = pltpu.make_async_remote_copy(
            src_ref=slab,
            dst_ref=slab,
            send_sem=pass_send.at[mask],
            recv_sem=pass_recv.at[mask],
            device_id={"groups": 1 - group},
            device_id_type=pl.DeviceIdType.MESH,
        )
        passed[mask].start()
    for mask in issue:
        passed[mask].wait()

    @pl.loop(0, count)
    def _(place):
        for parity in range(2):
            columns = pl.ds(pl.multiple_of((2 * place + parity) * block, block), block)
            re, im = signal[0:half, columns], signal[half : 2 * half, columns]
            filter_re = got_filter[0, parity, place].astype(jnp.float32)
            filter_im = got_filter[1, parity, place].astype(jnp.float32)
            for rows, item in (
                (slice(0, half), re * filter_re - im * filter_im),
                (slice(half, 2 * half), re * filter_im + im * filter_re),
            ):
                high = item.astype(jnp.bfloat16)
                wave_high[rows, columns] = high
                wave_low[rows, columns] = (item - high.astype(jnp.float32)).astype(jnp.bfloat16)

    @pl.loop(0, steps)
    def _(step):
        columns = pl.ds(pl.multiple_of(step * width, width), width)
        signal[:, columns] = product(2, columns)

    scale = 1.0 / (2 * count * tokens)

    @pl.loop(0, tokens // tile)
    def _(step):
        here = pl.ds(pl.multiple_of(step * tile, tile), tile)
        there = pl.ds(pl.multiple_of(half + step * tile, tile), tile)
        total = None
        for parity in range(2):
            waves = [None] * count
            for place in range(count):
                column = 2 * place + parity
                columns = slice(column * block, (column + 1) * block)
                re, im = signal[here, columns], signal[there, columns]
                cos = twist_ref[here, column : column + 1]
                sin = twist_ref[here, 2 * count + column : 2 * count + column + 1]
                waves[reverse(place)] = (re * cos + im * sin, im * cos - re * sin)
            pairs = short_transform(waves, 1)
            parts = [times_root(pair, source * parity, 2 * count)[0] for source, pair in enumerate(pairs)]
            total = parts if total is None else [left + right for left, right in zip(total, parts)]
        for source in range(count):
            result[source, here, :] = (total[source] * scale).astype(jnp.bfloat16)

    out_ref[:, lanes(device)] = result[device]
    returned = {}
    for mask in issue:
        returned[mask] = to_peer(2, mask, result.at[peers[mask]], out_ref.at[:, lanes(device)])
        returned[mask].start()
    for mask in issue:
        returned[mask].wait()


def run_convolution(value_stream, filter_spectrum):
    tokens, channels = value_stream.shape
    count = len(MASKS)
    block = channels // count
    vmem = pl.BlockSpec(memory_space=pltpu.VMEM)
    bf16 = jnp.bfloat16
    return pl.pallas_call(
        conv_kernel,
        out_shape=jax.ShapeDtypeStruct((tokens, channels), bf16),
        in_specs=[vmem, pl.BlockSpec(memory_space=pl.ANY), vmem, vmem],
        out_specs=vmem,
        scratch_shapes=[
            pltpu.VMEM((count, tokens, block), bf16),
            pltpu.VMEM((2, 2, count, tokens, block), bf16),
            pltpu.VMEM((2 * tokens, 2 * channels), bf16),
            pltpu.VMEM((2 * tokens, 2 * channels), bf16),
            pltpu.VMEM((2 * tokens, 2 * channels), jnp.float32),
            pltpu.VMEM((count, tokens, block), bf16),
            pltpu.SemaphoreType.DMA((2,)),
            pltpu.SemaphoreType.DMA((3, count)),
            pltpu.SemaphoreType.DMA((3, count)),
            pltpu.SemaphoreType.DMA((count,)),
            pltpu.SemaphoreType.DMA((count,)),
        ],
        compiler_params=pltpu.CompilerParams(
            collective_id=2, has_side_effects=True, vmem_limit_bytes=48 * 1024 * 1024
        ),
    )(value_stream, filter_spectrum, inner_tables(tokens), twist_table(count, tokens))


def expert_kernel(
    conv_ref, stream_ref, router_ref, ids_ref, head_ref, tail_ref, wg_hbm, wu_hbm, wd_hbm, out_ref,
    hyena, send_head, send_tail, recv_head, recv_tail, done_head, done_tail, back_head, back_tail,
    rows, hidden, wg, wu, wd, tail_sum, gates, own_sem, send_sem, recv_sem, weight_sem,
):
    device = lax.axis_index("ctx")
    peers = [flip_bits(device, mask) for mask in MASKS]
    count = len(MASKS)
    channels = conv_ref.shape[1]
    quarter = channels // QUARTERS
    tokens = conv_ref.shape[0]
    slots = count * HEAD
    weights = [
        pltpu.make_async_copy(src, dst, weight_sem.at[i])
        for i, (src, dst) in enumerate(((wg_hbm, wg), (wu_hbm, wu), (wd_hbm, wd)))
    ]
    for copy in weights:
        copy.start()
    barrier = pltpu.get_barrier_semaphore()
    for slot in range(1, count):
        pl.semaphore_signal(
            barrier, inc=1, device_id={"ctx": peers[slot]}, device_id_type=pl.DeviceIdType.MESH
        )
    mixed = (stream_ref[...].astype(jnp.float32) * conv_ref[...].astype(jnp.float32)).astype(jnp.bfloat16)
    hyena[...] = mixed
    mixed32 = mixed.astype(jnp.float32)
    mean = jnp.sum(mixed32 * mixed32, axis=1, keepdims=True) / channels
    normed = (mixed32 * lax.rsqrt(mean + 1e-06)).astype(jnp.bfloat16)
    slot_row = lax.broadcasted_iota(jnp.int32, (slots, tokens), 0)

    def hits(targets, shift):
        return [slot_row == targets[pick : pick + 1, :] + shift for pick in range(2)]

    def one_hot(targets, shift):
        first, second = hits(targets, shift)
        return jnp.where(first | second, 1.0, 0.0).astype(jnp.bfloat16)

    head = head_ref[...]
    tail = tail_ref[...]
    send_head[...] = jnp.dot(one_hot(head, 0), normed, preferred_element_type=jnp.float32).astype(jnp.bfloat16)
    packed = jnp.zeros((slots, quarter), jnp.float32)
    for part in range(QUARTERS):
        packed = packed + jnp.dot(
            one_hot(tail, TAIL * part),
            normed[:, part * quarter : (part + 1) * quarter],
            preferred_element_type=jnp.float32,
        )
    send_tail[...] = packed.astype(jnp.bfloat16)
    pl.semaphore_wait(barrier, count - 1)

    def exchange(slot, phase):
        here = pl.ds(slot * HEAD, HEAD)
        if phase == 0:
            pairs = ((send_head, recv_head), (send_tail, recv_tail))
        else:
            pairs = ((done_head, back_head), (done_tail, back_tail))
        copies = []
        for which, (src, dst) in enumerate(pairs):
            if slot == 0:
                copies.append(pltpu.make_async_copy(src.at[here], dst.at[here], own_sem.at[phase, which]))
            else:
                copies.append(
                    pltpu.make_async_remote_copy(
                        src_ref=src.at[here],
                        dst_ref=dst.at[here],
                        send_sem=send_sem.at[phase, which, slot],
                        recv_sem=recv_sem.at[phase, which, slot],
                        device_id={"ctx": peers[slot]},
                        device_id_type=pl.DeviceIdType.MESH,
                    )
                )
        return copies

    half = count // 2
    issue = (7, 6, 5, 4, 3, 2, 1, 0, 15, 14, 13, 12, 11, 10, 9, 8)
    outward = {slot: exchange(slot, 0) for slot in range(count)}
    inward = {slot: exchange(slot, 1) for slot in range(count)}
    for slot in issue:
        for copy in outward[slot]:
            copy.start()
    logits = lax.dot_general(
        router_ref[...], normed, (((1,), (1,)), ((), ())), preferred_element_type=jnp.float32
    )
    expert_row = lax.broadcasted_iota(jnp.int32, logits.shape, 0)
    ids = ids_ref[...]
    for pick in range(2):
        chosen = jnp.sum(
            jnp.where(expert_row == ids[pick : pick + 1, :], logits, 0.0), axis=0, keepdims=True
        )
        gates[pick : pick + 1, :] = jax.nn.sigmoid(chosen)
    group_rows = half * HEAD
    tail_rows = half * TAIL
    pick_row = lax.broadcasted_iota(jnp.int32, (tail_rows, group_rows), 0)
    pick_col = lax.broadcasted_iota(jnp.int32, (tail_rows, group_rows), 1)
    pick_base = (pick_row // TAIL) * HEAD + pick_row % TAIL
    hidden_size = wg.shape[1]
    for group in range(2):
        for slot in range(group * half, (group + 1) * half):
            for copy in outward[slot]:
                copy.wait()
        span = pl.ds(group * group_rows, group_rows)
        rows[0:group_rows, :] = recv_head[span, :]
        for part in range(QUARTERS):
            select = jnp.where(pick_col == pick_base + TAIL * part, 1.0, 0.0).astype(jnp.bfloat16)
            rows[group_rows : group_rows + tail_rows, part * quarter : (part + 1) * quarter] = jnp.dot(
                select, recv_tail[span, :], preferred_element_type=jnp.float32
            ).astype(jnp.bfloat16)
        if group == 0:
            weights[0].wait()
            weights[1].wait()

        @pl.loop(0, hidden_size // 256)
        def _(step):
            columns = pl.ds(pl.multiple_of(step * 256, 256), 256)
            gate_part = jnp.dot(rows[...], wg[:, columns], preferred_element_type=jnp.float32)
            up_part = jnp.dot(rows[...], wu[:, columns], preferred_element_type=jnp.float32)
            hidden[:, columns] = (jax.nn.silu(gate_part) * up_part).astype(jnp.bfloat16)

        if group == 0:
            weights[2].wait()
        tail_sum[...] = jnp.zeros_like(tail_sum)

        @pl.loop(0, QUARTERS)
        def _(part):
            columns = pl.ds(pl.multiple_of(part * quarter, 256), quarter)
            value = jnp.dot(hidden[...], wd[:, columns], preferred_element_type=jnp.float32).astype(jnp.bfloat16)
            done_head[span, columns] = value[0:group_rows, :]
            select = jnp.where(pick_col == pick_base + TAIL * part, 1.0, 0.0).astype(jnp.bfloat16)
            tail_sum[...] += lax.dot_general(
                select,
                value[group_rows : group_rows + tail_rows, :],
                (((0,), (0,)), ((), ())),
                preferred_element_type=jnp.float32,
            )

        done_tail[span, :] = tail_sum[...].astype(jnp.bfloat16)
        for slot in issue[group * half : (group + 1) * half]:
            for copy in inward[slot]:
                copy.start()

    def weighted(targets, shift, values):
        first, second = hits(targets, shift)
        mix = jnp.where(first, gates[0:1, :], 0.0) + jnp.where(second, gates[1:2, :], 0.0)
        high = mix.astype(jnp.bfloat16)
        low = (mix - high.astype(jnp.float32)).astype(jnp.bfloat16)
        dims = (((0,), (0,)), ((), ()))
        return lax.dot_general(high, values, dims, preferred_element_type=jnp.float32) + lax.dot_general(
            low, values, dims, preferred_element_type=jnp.float32
        )

    for slot in range(count):
        for copy in inward[slot]:
            copy.wait()
    for part in range(QUARTERS):
        columns = slice(part * quarter, (part + 1) * quarter)
        total = hyena[:, columns].astype(jnp.float32)
        total = total + weighted(head, 0, back_head[:, columns])
        total = total + weighted(tail, TAIL * part, back_tail[...])
        out_ref[:, columns] = total.astype(jnp.bfloat16)


def run_experts(long_conv, gate_stream, router, w_gate, w_up, w_down, route_ids, route_slots):
    tokens, channels = gate_stream.shape
    hidden_size = w_gate.shape[1]
    count = len(MASKS)
    slots = count * HEAD
    half_rows = slots // 2 + (count // 2) * TAIL
    quarter = channels // QUARTERS
    device = lax.axis_index("ctx")
    place = jnp.asarray(np.argsort(np.asarray(MASKS)), jnp.int32)
    offset = jnp.bitwise_xor(route_ids, device)
    position = jnp.sum(
        jnp.where(offset[:, :, None] == jnp.arange(count)[None, None, :], place[None, None, :], 0), axis=2
    )
    head = jnp.where(route_slots < HEAD, position * HEAD + route_slots, -1024)
    tail = jnp.where(
        (route_slots >= HEAD) & (route_slots < CAP), position * HEAD + route_slots - HEAD, -1024
    )
    vmem = pl.BlockSpec(memory_space=pltpu.VMEM)
    hbm = pl.BlockSpec(memory_space=pl.ANY)
    bf16 = jnp.bfloat16
    return pl.pallas_call(
        expert_kernel,
        out_shape=jax.ShapeDtypeStruct((tokens, channels), bf16),
        in_specs=[vmem] * 6 + [hbm] * 3,
        out_specs=vmem,
        scratch_shapes=[pltpu.VMEM((tokens, channels), bf16)]
        + [pltpu.VMEM((slots, channels), bf16), pltpu.VMEM((slots, quarter), bf16)] * 4
        + [
            pltpu.VMEM((half_rows, channels), bf16),
            pltpu.VMEM((half_rows, hidden_size), bf16),
            pltpu.VMEM((channels, hidden_size), bf16),
            pltpu.VMEM((channels, hidden_size), bf16),
            pltpu.VMEM((hidden_size, channels), bf16),
            pltpu.VMEM((slots // 2, quarter), jnp.float32),
            pltpu.VMEM((8, tokens), jnp.float32),
            pltpu.SemaphoreType.DMA((2, 2)),
            pltpu.SemaphoreType.DMA((2, 2, count)),
            pltpu.SemaphoreType.DMA((2, 2, count)),
            pltpu.SemaphoreType.DMA((3,)),
        ],
        compiler_params=pltpu.CompilerParams(
            collective_id=1, has_side_effects=True, vmem_limit_bytes=56 * 1024 * 1024
        ),
    )(long_conv, gate_stream, router.T, route_ids, head, tail, w_gate, w_up, w_down)


def local(
    value_stream, gate_stream, filter_spectrum, router, w_gate, w_up, w_down, route_ids, route_slots
):
    tok_rows, channels = value_stream.shape
    size_ctx = lax.axis_size("ctx")
    block = channels // size_ctx
    expert_count = router.shape[1]
    if (
        size_ctx == expert_count == len(MASKS)
        and lax.axis_size("groups") == 2
        and block == tok_rows == 128
        and w_gate.shape[1] % 256 == 0
    ):
        long_conv = run_convolution(value_stream, filter_spectrum)
        return run_experts(
            long_conv, gate_stream, router, w_gate, w_up, w_down, route_ids, route_slots
        )
    arrived = lax.all_to_all(value_stream, "ctx", split_axis=1, concat_axis=0, tiled=True)
    filter_all = lax.all_to_all(filter_spectrum, "ctx", split_axis=3, concat_axis=2, tiled=True)
    long_conv = convolve(arrived, filter_all, size_ctx, tok_rows, block)
    long_conv = lax.all_to_all(
        long_conv.astype(jnp.bfloat16), "ctx", split_axis=0, concat_axis=1, tiled=True
    )
    long_conv = long_conv.astype(jnp.float32)
    hyena_out = (gate_stream.astype(jnp.float32) * long_conv).astype(jnp.bfloat16)
    hyena32 = hyena_out.astype(jnp.float32)
    inv_rms = lax.rsqrt(jnp.mean(hyena32 * hyena32, axis=1, keepdims=True) + 1e-06)
    normed = (hyena32 * inv_rms).astype(jnp.bfloat16)
    logits = jnp.dot(normed, router, preferred_element_type=jnp.float32)
    owner_split = size_ctx // expert_count
    slot_count = expert_count * CAP
    positions = jnp.arange(slot_count, dtype=jnp.int32)
    expert_range = jnp.arange(expert_count, dtype=jnp.int32)
    combine = jnp.zeros((tok_rows, slot_count), jnp.float32)
    dispatch = jnp.zeros((slot_count, channels), jnp.float32)
    for pick_index in range(route_ids.shape[0]):
        expert_ids = route_ids[pick_index]
        slot_ids = route_slots[pick_index]
        target = jnp.where(slot_ids < CAP, expert_ids * CAP + slot_ids, -1)
        slot_hits = target[:, None] == positions[None, :]
        chosen_logit = jnp.sum(
            jnp.where(expert_ids[:, None] == expert_range[None, :], logits, 0.0), axis=1
        )
        gate_value = jax.nn.sigmoid(chosen_logit)
        combine = combine + slot_hits.astype(jnp.float32) * gate_value[:, None]
        dispatch = dispatch + lax.dot_general(
            slot_hits.astype(jnp.bfloat16),
            normed,
            (((0,), (0,)), ((), ())),
            preferred_element_type=jnp.float32,
        )
    buffer = dispatch.astype(jnp.bfloat16).reshape(expert_count, CAP, channels)
    outgoing = jnp.repeat(buffer, owner_split, axis=0)
    slot_rows = lax.all_to_all(outgoing, "ctx", split_axis=0, concat_axis=0, tiled=True)
    flat_rows = slot_rows.reshape(-1, channels)
    gate_part = jnp.dot(flat_rows, w_gate, preferred_element_type=jnp.float32)
    up_part = jnp.dot(flat_rows, w_up, preferred_element_type=jnp.float32)
    hidden = (jax.nn.silu(gate_part) * up_part).astype(jnp.bfloat16)
    partial_value = jnp.dot(hidden, w_down, preferred_element_type=jnp.float32).astype(jnp.bfloat16)
    returned = lax.all_to_all(
        partial_value.reshape(slot_rows.shape), "ctx", split_axis=0, concat_axis=0, tiled=True
    )
    expert_out = jnp.sum(
        returned.astype(jnp.float32).reshape(expert_count, owner_split, CAP, channels), axis=1
    ).reshape(slot_count, channels)
    contribution = jnp.dot(combine, expert_out, precision=highest)
    return (hyena32 + contribution).astype(jnp.bfloat16)


def solution(mesh):
    in_specs = (
        P(("groups", "ctx"), None),
        P(("groups", "ctx"), None),
        P(None, None, "ctx", None),
        P(),
        P(None, "ctx"),
        P(None, "ctx"),
        P("ctx", None),
        P(None, ("groups", "ctx")),
        P(None, ("groups", "ctx")),
    )
    out_specs = P(("groups", "ctx"), None)
    return jax.shard_map(local, mesh=mesh, in_specs=in_specs, out_specs=out_specs, check_vma=False)
```

```python
import jax
import jax.numpy as jnp
import numpy as np
from jax import lax
from jax.experimental import pallas as pl
from jax.experimental.pallas import tpu as pltpu
from jax.sharding import PartitionSpec as P

CAP = 20


two_pi = 2.0 * np.pi
highest = lax.Precision.HIGHEST


def reverse_bits(length_n):
    bit_count = length_n.bit_length() - 1
    positions = np.arange(length_n)
    reversed_index = np.zeros(length_n, dtype=np.int64)
    for position in range(bit_count):
        reversed_index = reversed_index | (positions >> position & 1) << bit_count - 1 - position
    return reversed_index


def spread_table(size_ctx):
    rho = 2 * reverse_bits(size_ctx)[None, :] + np.arange(2)[:, None]
    angle_rad = -two_pi * (np.outer(rho.reshape(-1), np.arange(size_ctx)) % (2 * size_ctx)) / (2 * size_ctx)
    parts = np.stack([np.cos(angle_rad), np.sin(angle_rad)], axis=1)
    return jnp.asarray(parts, jnp.float32)


def fine_table(size_ctx, tok_rows):
    total = 2 * size_ctx * tok_rows
    rho = (2 * reverse_bits(size_ctx)[None, :] + np.arange(2)[:, None]).reshape(-1)
    k = 2 * size_ctx * reverse_bits(tok_rows)[None, :] + rho[:, None]
    step = (k[:, :, None] * np.arange(tok_rows)[None, None, :]) % total
    angle_rad = -two_pi * step / total
    re, im = np.cos(angle_rad), np.sin(angle_rad)
    table = np.stack([np.stack([re, -im], axis=2), np.stack([im, re], axis=2)], axis=1)
    return jnp.asarray(table.reshape(2 * size_ctx, 2 * tok_rows, 2 * tok_rows), jnp.float32)


def convolve(arrived, filter_all, size_ctx, tok_rows, block):
    rho_count = 2 * size_ctx
    coarse = spread_table(size_ctx)
    fine = fine_table(size_ctx, tok_rows)
    samples = arrived.astype(jnp.float32).reshape(size_ctx, tok_rows * block)
    spread = jnp.dot(coarse.reshape(2 * rho_count, size_ctx), samples, precision=highest)
    spread = spread.reshape(rho_count, 2 * tok_rows, block)
    signal = jnp.einsum("rqt,rtc->rqc", fine, spread, precision=highest)
    signal = signal.reshape(rho_count, 2, tok_rows, block)
    filter32 = filter_all.astype(jnp.float32).reshape(2, rho_count, tok_rows, block)
    real_part = signal[:, 0] * filter32[0] - signal[:, 1] * filter32[1]
    imag_part = signal[:, 0] * filter32[1] + signal[:, 1] * filter32[0]
    signal = jnp.concatenate([real_part, imag_part], axis=1)
    spread = jnp.einsum("rqt,rqc->rtc", fine, signal, precision=highest)
    spread = spread.reshape(2 * rho_count, tok_rows * block)
    folded = jnp.dot(coarse.reshape(2 * rho_count, size_ctx).T, spread, precision=highest)
    return (folded / (rho_count * tok_rows)).reshape(size_ctx * tok_rows, block)


def flip_bits(index, mask):
    result = index
    bit = 1
    while bit <= mask:
        if mask & bit:
            result = result + bit * (1 - 2 * ((index // bit) % 2))
        bit *= 2
    return result


MASKS = (0, 1, 2, 3, 8, 9, 10, 11, 4, 5, 6, 7, 12, 13, 14, 15)
HEAD = 16
TAIL = CAP - HEAD
QUARTERS = HEAD // TAIL


def twist_table(size_ctx, tok_rows):
    rho = (2 * reverse_bits(size_ctx)[:, None] + np.arange(2)[None, :]).reshape(-1)
    angle_rad = -two_pi * np.outer(np.arange(tok_rows), rho) / (2 * size_ctx * tok_rows)
    return jnp.asarray(np.concatenate([np.cos(angle_rad), np.sin(angle_rad)], axis=1), jnp.float32)


def inner_tables(tok_rows):
    angle_rad = -two_pi * (np.outer(reverse_bits(tok_rows), np.arange(tok_rows)) % tok_rows) / tok_rows
    re, im = np.cos(angle_rad), np.sin(angle_rad)
    table = np.block([[re, -im], [im, re]]).astype(np.float32)
    pieces = []
    for matrix in (table, table.T):
        high = matrix.astype(jnp.bfloat16)
        low = (matrix - high.astype(np.float32)).astype(jnp.bfloat16)
        pieces += [high, low]
    return jnp.asarray(np.stack(pieces))


def times_root(pair, power, order):
    power %= order
    re, im = pair
    if power == 0:
        return pair
    if im is None and 4 * power % order:
        cos, sin = float(np.cos(two_pi * power / order)), float(np.sin(two_pi * power / order))
        return (re * cos, re * sin)
    if im is None:
        im = jnp.zeros_like(re)
    if 4 * power == order:
        return (-im, re)
    if 2 * power == order:
        return (-re, -im)
    if 4 * power == 3 * order:
        return (im, -re)
    cos, sin = float(np.cos(two_pi * power / order)), float(np.sin(two_pi * power / order))
    return (re * cos - im * sin, re * sin + im * cos)


def short_transform(values, sign):
    order = len(values)
    if order == 1:
        return values
    even = short_transform(values[0::2], sign)
    odd = short_transform(values[1::2], sign)
    turned = [times_root(odd[i], sign * i, order) for i in range(order // 2)]
    return [(even[i][0] + turned[i][0], even[i][1] + turned[i][1]) for i in range(order // 2)] + [
        (even[i][0] - turned[i][0], even[i][1] - turned[i][1]) for i in range(order // 2)
    ]


def conv_kernel(
    values_ref, filter_ref, tables_hbm, twist_hbm, out_ref,
    tables_ref, twist_ref, got_values, got_filter, wave_high, wave_low, signal, result,
    own_sem, send_sem, recv_sem, pass_send, pass_recv,
):
    device = lax.axis_index("ctx")
    group = lax.axis_index("groups")
    count = len(MASKS)
    tokens = values_ref.shape[0]
    block = values_ref.shape[1] // count
    peers = [flip_bits(device, mask) for mask in range(count)]
    barrier = pltpu.get_barrier_semaphore()
    for mask in range(1, count):
        pl.semaphore_signal(
            barrier, inc=1, device_id={"ctx": peers[mask]}, device_id_type=pl.DeviceIdType.MESH
        )
    pl.semaphore_signal(
        barrier, inc=1, device_id={"groups": 1 - group}, device_id_type=pl.DeviceIdType.MESH
    )

    def lanes(index):
        return pl.ds(pl.multiple_of(index * block, block), block)

    def to_peer(kind, mask, src, dst):
        return pltpu.make_async_remote_copy(
            src_ref=src,
            dst_ref=dst,
            send_sem=send_sem.at[kind, mask],
            recv_sem=recv_sem.at[kind, mask],
            device_id={"ctx": peers[mask]},
            device_id_type=pl.DeviceIdType.MESH,
        )

    own = [
        pltpu.make_async_copy(values_ref.at[:, lanes(device)], got_values.at[device], own_sem.at[0]),
        pltpu.make_async_copy(
            filter_ref.at[:, :, :, lanes(device)], got_filter.at[:, :, device], own_sem.at[1]
        ),
    ]
    own += [
        pltpu.make_async_copy(tables_hbm, tables_ref, own_sem.at[2]),
        pltpu.make_async_copy(twist_hbm, twist_ref, own_sem.at[3]),
    ]
    pl.semaphore_wait(barrier, count)
    issue = (15, 14, 13, 12, 11, 10, 9, 8, 7, 6, 5, 4, 3, 2, 1)
    sent_values, sent_filter, passed = {}, {}, {}
    for mask in issue:
        sent_filter[mask] = to_peer(
            1, mask, filter_ref.at[:, group, :, lanes(peers[mask])], got_filter.at[:, group, device]
        )
        sent_filter[mask].start()
    for mask in issue:
        sent_values[mask] = to_peer(
            0, mask, values_ref.at[:, lanes(peers[mask])], got_values.at[device]
        )
        sent_values[mask].start()
    for copy in own:
        copy.start()
    for mask in issue:
        sent_filter[mask].wait_recv()
        slab = got_filter.at[:, group, peers[mask]]
        passed[mask] = pltpu.make_async_remote_copy(
            src_ref=slab,
            dst_ref=slab,
            send_sem=pass_send.at[mask],
            recv_sem=pass_recv.at[mask],
            device_id={"groups": 1 - group},
            device_id_type=pl.DeviceIdType.MESH,
        )
        passed[mask].start()
    for copy in own:
        copy.wait()
    for mask in issue:
        sent_values[mask].wait_recv()

    def reverse(index):
        return int(reverse_bits(count)[index])

    half = tokens
    tile = 16

    @pl.loop(0, tokens // tile)
    def _(step):
        here = pl.ds(pl.multiple_of(step * tile, tile), tile)
        there = pl.ds(pl.multiple_of(half + step * tile, tile), tile)
        samples = [got_values[source, here, :].astype(jnp.float32) for source in range(count)]
        zero = jnp.zeros_like(samples[0])
        for parity in range(2):
            pairs = [
                times_root((item, None), -source * parity, 2 * count)
                for source, item in enumerate(samples)
            ]
            pairs = [(re, zero if im is None else im) for re, im in pairs]
            waves = short_transform(pairs, -1)
            for place in range(count):
                re, im = waves[reverse(place)]
                column = 2 * place + parity
                cos = twist_ref[here, column : column + 1]
                sin = twist_ref[here, 2 * count + column : 2 * count + column + 1]
                for rows, item in ((here, re * cos - im * sin), (there, re * sin + im * cos)):
                    high = item.astype(jnp.bfloat16)
                    columns = slice(column * block, (column + 1) * block)
                    wave_high[rows, columns] = high
                    wave_low[rows, columns] = (item - high.astype(jnp.float32)).astype(jnp.bfloat16)

    width = 4 * block

    def product(which, columns):
        high, low = wave_high[:, columns], wave_low[:, columns]
        return (
            jnp.dot(tables_ref[which], high, preferred_element_type=jnp.float32)
            + jnp.dot(tables_ref[which], low, preferred_element_type=jnp.float32)
            + jnp.dot(tables_ref[which + 1], high, preferred_element_type=jnp.float32)
        )

    steps = 2 * count * block // width

    @pl.loop(0, steps)
    def _(step):
        columns = pl.ds(pl.multiple_of(step * width, width), width)
        signal[:, columns] = product(0, columns)

    for mask in issue:
        passed[mask].wait_recv()

    @pl.loop(0, count)
    def _(place):
        for parity in range(2):
            columns = pl.ds(pl.multiple_of((2 * place + parity) * block, block), block)
            re, im = signal[0:half, columns], signal[half : 2 * half, columns]
            filter_re = got_filter[0, parity, place].astype(jnp.float32)
            filter_im = got_filter[1, parity, place].astype(jnp.float32)
            for rows, item in (
                (slice(0, half), re * filter_re - im * filter_im),
                (slice(half, 2 * half), re * filter_im + im * filter_re),
            ):
                high = item.astype(jnp.bfloat16)
                wave_high[rows, columns] = high
                wave_low[rows, columns] = (item - high.astype(jnp.float32)).astype(jnp.bfloat16)

    @pl.loop(0, steps)
    def _(step):
        columns = pl.ds(pl.multiple_of(step * width, width), width)
        signal[:, columns] = product(2, columns)

    scale = 1.0 / (2 * count * tokens)

    @pl.loop(0, tokens // tile)
    def _(step):
        here = pl.ds(pl.multiple_of(step * tile, tile), tile)
        there = pl.ds(pl.multiple_of(half + step * tile, tile), tile)
        total = None
        for parity in range(2):
            waves = [None] * count
            for place in range(count):
                column = 2 * place + parity
                columns = slice(column * block, (column + 1) * block)
                re, im = signal[here, columns], signal[there, columns]
                cos = twist_ref[here, column : column + 1]
                sin = twist_ref[here, 2 * count + column : 2 * count + column + 1]
                waves[reverse(place)] = (re * cos + im * sin, im * cos - re * sin)
            pairs = short_transform(waves, 1)
            parts = [times_root(pair, source * parity, 2 * count)[0] for source, pair in enumerate(pairs)]
            total = parts if total is None else [left + right for left, right in zip(total, parts)]
        for source in range(count):
            result[source, here, :] = (total[source] * scale).astype(jnp.bfloat16)

    out_ref[:, lanes(device)] = result[device]
    returned = {}
    for mask in issue:
        returned[mask] = to_peer(2, mask, result.at[peers[mask]], out_ref.at[:, lanes(device)])
        returned[mask].start()
    for mask in issue:
        returned[mask].wait()
        passed[mask].wait_send()
        sent_values[mask].wait_send()
        sent_filter[mask].wait_send()


def run_convolution(value_stream, filter_spectrum):
    tokens, channels = value_stream.shape
    count = len(MASKS)
    block = channels // count
    vmem = pl.BlockSpec(memory_space=pltpu.VMEM)
    bf16 = jnp.bfloat16
    return pl.pallas_call(
        conv_kernel,
        out_shape=jax.ShapeDtypeStruct((tokens, channels), bf16),
        in_specs=[pl.BlockSpec(memory_space=pl.ANY)] * 4,
        out_specs=vmem,
        scratch_shapes=[
            pltpu.VMEM((4, 2 * tokens, 2 * tokens), bf16),
            pltpu.VMEM((tokens, 4 * count), jnp.float32),
            pltpu.VMEM((count, tokens, block), bf16),
            pltpu.VMEM((2, 2, count, tokens, block), bf16),
            pltpu.VMEM((2 * tokens, 2 * channels), bf16),
            pltpu.VMEM((2 * tokens, 2 * channels), bf16),
            pltpu.VMEM((2 * tokens, 2 * channels), jnp.float32),
            pltpu.VMEM((count, tokens, block), bf16),
            pltpu.SemaphoreType.DMA((4,)),
            pltpu.SemaphoreType.DMA((3, count)),
            pltpu.SemaphoreType.DMA((3, count)),
            pltpu.SemaphoreType.DMA((count,)),
            pltpu.SemaphoreType.DMA((count,)),
        ],
        compiler_params=pltpu.CompilerParams(
            collective_id=2, has_side_effects=True, vmem_limit_bytes=48 * 1024 * 1024
        ),
    )(value_stream, filter_spectrum, inner_tables(tokens), twist_table(count, tokens))


def expert_kernel(
    conv_ref, stream_hbm, router_ref, ids_ref, slots_ref, wg_hbm, wu_hbm, wd_hbm, out_ref,
    stream_ref, hyena, send_head, send_tail, recv_head, recv_tail, done_head, done_tail, back_head, back_tail,
    rows, hidden, wg, wu, wd, tail_sum, gates, own_sem, send_sem, recv_sem, weight_sem,
):
    device = lax.axis_index("ctx")
    peers = [flip_bits(device, mask) for mask in MASKS]
    count = len(MASKS)
    channels = conv_ref.shape[1]
    quarter = channels // QUARTERS
    tokens = conv_ref.shape[0]
    slots = count * HEAD
    weights = [
        pltpu.make_async_copy(src, dst, weight_sem.at[i])
        for i, (src, dst) in enumerate(((wg_hbm, wg), (wu_hbm, wu), (wd_hbm, wd)))
    ]
    stream_copy = pltpu.make_async_copy(stream_hbm, stream_ref, weight_sem.at[3])
    stream_copy.start()
    barrier = pltpu.get_barrier_semaphore()
    for slot in range(1, count):
        pl.semaphore_signal(
            barrier, inc=1, device_id={"ctx": peers[slot]}, device_id_type=pl.DeviceIdType.MESH
        )
    for copy in weights:
        copy.start()
    ids = ids_ref[...]
    picks = slots_ref[...]
    position = jnp.zeros_like(ids)
    for slot in range(count):
        position = jnp.where(ids == peers[slot], slot, position)
    head = jnp.where(picks < HEAD, position * HEAD + picks, -1024)
    tail = jnp.where((picks >= HEAD) & (picks < CAP), position * HEAD + picks - HEAD, -1024)
    stream_copy.wait()
    mixed = (stream_ref[...].astype(jnp.float32) * conv_ref[...].astype(jnp.float32)).astype(jnp.bfloat16)
    hyena[...] = mixed
    mixed32 = mixed.astype(jnp.float32)
    mean = jnp.sum(mixed32 * mixed32, axis=1, keepdims=True) / channels
    normed = (mixed32 * lax.rsqrt(mean + 1e-06)).astype(jnp.bfloat16)
    slot_row = lax.broadcasted_iota(jnp.int32, (slots, tokens), 0)

    def hits(targets, shift):
        return [slot_row == targets[pick : pick + 1, :] + shift for pick in range(2)]

    def one_hot(targets, shift):
        first, second = hits(targets, shift)
        return jnp.where(first | second, 1.0, 0.0).astype(jnp.bfloat16)

    send_head[...] = jnp.dot(one_hot(head, 0), normed, preferred_element_type=jnp.float32).astype(jnp.bfloat16)
    packed = jnp.zeros((slots, quarter), jnp.float32)
    for part in range(QUARTERS):
        packed = packed + jnp.dot(
            one_hot(tail, TAIL * part),
            normed[:, part * quarter : (part + 1) * quarter],
            preferred_element_type=jnp.float32,
        )
    send_tail[...] = packed.astype(jnp.bfloat16)
    pl.semaphore_wait(barrier, count - 1)

    def exchange(slot, phase):
        here = pl.ds(slot * HEAD, HEAD)
        if phase == 0:
            pairs = ((send_head, recv_head), (send_tail, recv_tail))
        else:
            pairs = ((done_head, back_head), (done_tail, back_tail))
        copies = []
        for which, (src, dst) in enumerate(pairs):
            if slot == 0:
                copies.append(pltpu.make_async_copy(src.at[here], dst.at[here], own_sem.at[phase, which]))
            else:
                copies.append(
                    pltpu.make_async_remote_copy(
                        src_ref=src.at[here],
                        dst_ref=dst.at[here],
                        send_sem=send_sem.at[phase, which, slot],
                        recv_sem=recv_sem.at[phase, which, slot],
                        device_id={"ctx": peers[slot]},
                        device_id_type=pl.DeviceIdType.MESH,
                    )
                )
        return copies

    half = count // 2
    issue = (7, 6, 5, 4, 3, 2, 1, 0, 15, 14, 13, 12, 11, 10, 9, 8)
    outward = {slot: exchange(slot, 0) for slot in range(count)}
    inward = {slot: exchange(slot, 1) for slot in range(count)}
    for slot in issue:
        for copy in outward[slot]:
            copy.start()
    logits = lax.dot_general(
        router_ref[...], normed, (((1,), (1,)), ((), ())), preferred_element_type=jnp.float32
    )
    expert_row = lax.broadcasted_iota(jnp.int32, logits.shape, 0)
    for pick in range(2):
        chosen = jnp.sum(
            jnp.where(expert_row == ids[pick : pick + 1, :], logits, 0.0), axis=0, keepdims=True
        )
        gates[pick : pick + 1, :] = jax.nn.sigmoid(chosen)
    group_rows = half * HEAD
    tail_rows = half * TAIL
    pick_row = lax.broadcasted_iota(jnp.int32, (tail_rows, group_rows), 0)
    pick_col = lax.broadcasted_iota(jnp.int32, (tail_rows, group_rows), 1)
    pick_base = (pick_row // TAIL) * HEAD + pick_row % TAIL
    hidden_size = wg.shape[1]
    for group in range(2):
        for slot in range(group * half, (group + 1) * half):
            for copy in outward[slot]:
                copy.wait()
        span = pl.ds(group * group_rows, group_rows)
        rows[0:group_rows, :] = recv_head[span, :]
        for part in range(QUARTERS):
            select = jnp.where(pick_col == pick_base + TAIL * part, 1.0, 0.0).astype(jnp.bfloat16)
            rows[group_rows : group_rows + tail_rows, part * quarter : (part + 1) * quarter] = jnp.dot(
                select, recv_tail[span, :], preferred_element_type=jnp.float32
            ).astype(jnp.bfloat16)
        if group == 0:
            weights[0].wait()
            weights[1].wait()

        @pl.loop(0, hidden_size // 256)
        def _(step):
            columns = pl.ds(pl.multiple_of(step * 256, 256), 256)
            gate_part = jnp.dot(rows[...], wg[:, columns], preferred_element_type=jnp.float32)
            up_part = jnp.dot(rows[...], wu[:, columns], preferred_element_type=jnp.float32)
            hidden[:, columns] = (jax.nn.silu(gate_part) * up_part).astype(jnp.bfloat16)

        if group == 0:
            weights[2].wait()
        tail_sum[...] = jnp.zeros_like(tail_sum)

        @pl.loop(0, QUARTERS)
        def _(part):
            columns = pl.ds(pl.multiple_of(part * quarter, 256), quarter)
            value = jnp.dot(hidden[...], wd[:, columns], preferred_element_type=jnp.float32).astype(jnp.bfloat16)
            done_head[span, columns] = value[0:group_rows, :]
            select = jnp.where(pick_col == pick_base + TAIL * part, 1.0, 0.0).astype(jnp.bfloat16)
            tail_sum[...] += lax.dot_general(
                select,
                value[group_rows : group_rows + tail_rows, :],
                (((0,), (0,)), ((), ())),
                preferred_element_type=jnp.float32,
            )

        done_tail[span, :] = tail_sum[...].astype(jnp.bfloat16)
        for slot in issue[group * half : (group + 1) * half]:
            for copy in inward[slot]:
                copy.start()

    def weighted(targets, shift, values):
        first, second = hits(targets, shift)
        mix = jnp.where(first, gates[0:1, :], 0.0) + jnp.where(second, gates[1:2, :], 0.0)
        high = mix.astype(jnp.bfloat16)
        low = (mix - high.astype(jnp.float32)).astype(jnp.bfloat16)
        dims = (((0,), (0,)), ((), ()))
        return lax.dot_general(high, values, dims, preferred_element_type=jnp.float32) + lax.dot_general(
            low, values, dims, preferred_element_type=jnp.float32
        )

    for slot in range(count):
        for copy in inward[slot]:
            copy.wait()
    for part in range(QUARTERS):
        columns = slice(part * quarter, (part + 1) * quarter)
        total = hyena[:, columns].astype(jnp.float32)
        total = total + weighted(head, 0, back_head[:, columns])
        total = total + weighted(tail, TAIL * part, back_tail[...])
        out_ref[:, columns] = total.astype(jnp.bfloat16)


def run_experts(long_conv, gate_stream, router, w_gate, w_up, w_down, route_ids, route_slots):
    tokens, channels = gate_stream.shape
    hidden_size = w_gate.shape[1]
    count = len(MASKS)
    slots = count * HEAD
    half_rows = slots // 2 + (count // 2) * TAIL
    quarter = channels // QUARTERS
    vmem = pl.BlockSpec(memory_space=pltpu.VMEM)
    hbm = pl.BlockSpec(memory_space=pl.ANY)
    bf16 = jnp.bfloat16
    return pl.pallas_call(
        expert_kernel,
        out_shape=jax.ShapeDtypeStruct((tokens, channels), bf16),
        in_specs=[vmem, hbm, vmem, vmem, vmem] + [hbm] * 3,
        out_specs=vmem,
        scratch_shapes=[pltpu.VMEM((tokens, channels), bf16)] * 2
        + [pltpu.VMEM((slots, channels), bf16), pltpu.VMEM((slots, quarter), bf16)] * 4
        + [
            pltpu.VMEM((half_rows, channels), bf16),
            pltpu.VMEM((half_rows, hidden_size), bf16),
            pltpu.VMEM((channels, hidden_size), bf16),
            pltpu.VMEM((channels, hidden_size), bf16),
            pltpu.VMEM((hidden_size, channels), bf16),
            pltpu.VMEM((slots // 2, quarter), jnp.float32),
            pltpu.VMEM((8, tokens), jnp.float32),
            pltpu.SemaphoreType.DMA((2, 2)),
            pltpu.SemaphoreType.DMA((2, 2, count)),
            pltpu.SemaphoreType.DMA((2, 2, count)),
            pltpu.SemaphoreType.DMA((4,)),
        ],
        compiler_params=pltpu.CompilerParams(
            collective_id=1, has_side_effects=True, vmem_limit_bytes=56 * 1024 * 1024
        ),
    )(long_conv, gate_stream, router.T, route_ids, route_slots, w_gate, w_up, w_down)


def local(
    value_stream, gate_stream, filter_spectrum, router, w_gate, w_up, w_down, route_ids, route_slots
):
    tok_rows, channels = value_stream.shape
    size_ctx = lax.axis_size("ctx")
    block = channels // size_ctx
    expert_count = router.shape[1]
    if (
        size_ctx == expert_count == len(MASKS)
        and lax.axis_size("groups") == 2
        and block == tok_rows == 128
        and w_gate.shape[1] % 256 == 0
    ):
        long_conv = run_convolution(value_stream, filter_spectrum)
        return run_experts(
            long_conv, gate_stream, router, w_gate, w_up, w_down, route_ids, route_slots
        )
    arrived = lax.all_to_all(value_stream, "ctx", split_axis=1, concat_axis=0, tiled=True)
    filter_all = lax.all_to_all(filter_spectrum, "ctx", split_axis=3, concat_axis=2, tiled=True)
    long_conv = convolve(arrived, filter_all, size_ctx, tok_rows, block)
    long_conv = lax.all_to_all(
        long_conv.astype(jnp.bfloat16), "ctx", split_axis=0, concat_axis=1, tiled=True
    )
    long_conv = long_conv.astype(jnp.float32)
    hyena_out = (gate_stream.astype(jnp.float32) * long_conv).astype(jnp.bfloat16)
    hyena32 = hyena_out.astype(jnp.float32)
    inv_rms = lax.rsqrt(jnp.mean(hyena32 * hyena32, axis=1, keepdims=True) + 1e-06)
    normed = (hyena32 * inv_rms).astype(jnp.bfloat16)
    logits = jnp.dot(normed, router, preferred_element_type=jnp.float32)
    owner_split = size_ctx // expert_count
    slot_count = expert_count * CAP
    positions = jnp.arange(slot_count, dtype=jnp.int32)
    expert_range = jnp.arange(expert_count, dtype=jnp.int32)
    combine = jnp.zeros((tok_rows, slot_count), jnp.float32)
    dispatch = jnp.zeros((slot_count, channels), jnp.float32)
    for pick_index in range(route_ids.shape[0]):
        expert_ids = route_ids[pick_index]
        slot_ids = route_slots[pick_index]
        target = jnp.where(slot_ids < CAP, expert_ids * CAP + slot_ids, -1)
        slot_hits = target[:, None] == positions[None, :]
        chosen_logit = jnp.sum(
            jnp.where(expert_ids[:, None] == expert_range[None, :], logits, 0.0), axis=1
        )
        gate_value = jax.nn.sigmoid(chosen_logit)
        combine = combine + slot_hits.astype(jnp.float32) * gate_value[:, None]
        dispatch = dispatch + lax.dot_general(
            slot_hits.astype(jnp.bfloat16),
            normed,
            (((0,), (0,)), ((), ())),
            preferred_element_type=jnp.float32,
        )
    buffer = dispatch.astype(jnp.bfloat16).reshape(expert_count, CAP, channels)
    outgoing = jnp.repeat(buffer, owner_split, axis=0)
    slot_rows = lax.all_to_all(outgoing, "ctx", split_axis=0, concat_axis=0, tiled=True)
    flat_rows = slot_rows.reshape(-1, channels)
    gate_part = jnp.dot(flat_rows, w_gate, preferred_element_type=jnp.float32)
    up_part = jnp.dot(flat_rows, w_up, preferred_element_type=jnp.float32)
    hidden = (jax.nn.silu(gate_part) * up_part).astype(jnp.bfloat16)
    partial_value = jnp.dot(hidden, w_down, preferred_element_type=jnp.float32).astype(jnp.bfloat16)
    returned = lax.all_to_all(
        partial_value.reshape(slot_rows.shape), "ctx", split_axis=0, concat_axis=0, tiled=True
    )
    expert_out = jnp.sum(
        returned.astype(jnp.float32).reshape(expert_count, owner_split, CAP, channels), axis=1
    ).reshape(slot_count, channels)
    contribution = jnp.dot(combine, expert_out, precision=highest)
    return (hyena32 + contribution).astype(jnp.bfloat16)


def solution(mesh):
    in_specs = (
        P(("groups", "ctx"), None),
        P(("groups", "ctx"), None),
        P(None, None, "ctx", None),
        P(),
        P(None, "ctx"),
        P(None, "ctx"),
        P("ctx", None),
        P(None, ("groups", "ctx")),
        P(None, ("groups", "ctx")),
    )
    out_specs = P(("groups", "ctx"), None)
    return jax.shard_map(local, mesh=mesh, in_specs=in_specs, out_specs=out_specs, check_vma=False)
```

```python
import jax
import jax.numpy as jnp
import numpy as np
from jax import lax
from jax.experimental import pallas as pl
from jax.experimental.pallas import tpu as pltpu
from jax.sharding import PartitionSpec as P

CAP = 20


two_pi = 2.0 * np.pi
highest = lax.Precision.HIGHEST


def reverse_bits(length_n):
    bit_count = length_n.bit_length() - 1
    positions = np.arange(length_n)
    reversed_index = np.zeros(length_n, dtype=np.int64)
    for position in range(bit_count):
        reversed_index = reversed_index | (positions >> position & 1) << bit_count - 1 - position
    return reversed_index


def spread_table(size_ctx):
    rho = 2 * reverse_bits(size_ctx)[None, :] + np.arange(2)[:, None]
    angle_rad = -two_pi * (np.outer(rho.reshape(-1), np.arange(size_ctx)) % (2 * size_ctx)) / (2 * size_ctx)
    parts = np.stack([np.cos(angle_rad), np.sin(angle_rad)], axis=1)
    return jnp.asarray(parts, jnp.float32)


def fine_table(size_ctx, tok_rows):
    total = 2 * size_ctx * tok_rows
    rho = (2 * reverse_bits(size_ctx)[None, :] + np.arange(2)[:, None]).reshape(-1)
    k = 2 * size_ctx * reverse_bits(tok_rows)[None, :] + rho[:, None]
    step = (k[:, :, None] * np.arange(tok_rows)[None, None, :]) % total
    angle_rad = -two_pi * step / total
    re, im = np.cos(angle_rad), np.sin(angle_rad)
    table = np.stack([np.stack([re, -im], axis=2), np.stack([im, re], axis=2)], axis=1)
    return jnp.asarray(table.reshape(2 * size_ctx, 2 * tok_rows, 2 * tok_rows), jnp.float32)


def convolve(arrived, filter_all, size_ctx, tok_rows, block):
    rho_count = 2 * size_ctx
    coarse = spread_table(size_ctx)
    fine = fine_table(size_ctx, tok_rows)
    samples = arrived.astype(jnp.float32).reshape(size_ctx, tok_rows * block)
    spread = jnp.dot(coarse.reshape(2 * rho_count, size_ctx), samples, precision=highest)
    spread = spread.reshape(rho_count, 2 * tok_rows, block)
    signal = jnp.einsum("rqt,rtc->rqc", fine, spread, precision=highest)
    signal = signal.reshape(rho_count, 2, tok_rows, block)
    filter32 = filter_all.astype(jnp.float32).reshape(2, rho_count, tok_rows, block)
    real_part = signal[:, 0] * filter32[0] - signal[:, 1] * filter32[1]
    imag_part = signal[:, 0] * filter32[1] + signal[:, 1] * filter32[0]
    signal = jnp.concatenate([real_part, imag_part], axis=1)
    spread = jnp.einsum("rqt,rqc->rtc", fine, signal, precision=highest)
    spread = spread.reshape(2 * rho_count, tok_rows * block)
    folded = jnp.dot(coarse.reshape(2 * rho_count, size_ctx).T, spread, precision=highest)
    return (folded / (rho_count * tok_rows)).reshape(size_ctx * tok_rows, block)


def flip_bits(index, mask):
    result = index
    bit = 1
    while bit <= mask:
        if mask & bit:
            result = result + bit * (1 - 2 * ((index // bit) % 2))
        bit *= 2
    return result


MASKS = (0, 1, 2, 3, 8, 9, 10, 11, 4, 5, 6, 7, 12, 13, 14, 15)
HEAD = 16
TAIL = CAP - HEAD
QUARTERS = HEAD // TAIL


def twist_table(size_ctx, tok_rows):
    rho = (2 * reverse_bits(size_ctx)[:, None] + np.arange(2)[None, :]).reshape(-1)
    angle_rad = -two_pi * np.outer(np.arange(tok_rows), rho) / (2 * size_ctx * tok_rows)
    return jnp.asarray(np.concatenate([np.cos(angle_rad), np.sin(angle_rad)], axis=1), jnp.float32)


def inner_tables(tok_rows):
    angle_rad = -two_pi * (np.outer(reverse_bits(tok_rows), np.arange(tok_rows)) % tok_rows) / tok_rows
    re, im = np.cos(angle_rad), np.sin(angle_rad)
    table = np.block([[re, -im], [im, re]]).astype(np.float32)
    pieces = []
    for matrix in (table, table.T):
        high = matrix.astype(jnp.bfloat16)
        low = (matrix - high.astype(np.float32)).astype(jnp.bfloat16)
        pieces += [high, low]
    return jnp.asarray(np.stack(pieces))


def times_root(pair, power, order):
    power %= order
    re, im = pair
    if power == 0:
        return pair
    if im is None and 4 * power % order:
        cos, sin = float(np.cos(two_pi * power / order)), float(np.sin(two_pi * power / order))
        return (re * cos, re * sin)
    if im is None:
        im = jnp.zeros_like(re)
    if 4 * power == order:
        return (-im, re)
    if 2 * power == order:
        return (-re, -im)
    if 4 * power == 3 * order:
        return (im, -re)
    cos, sin = float(np.cos(two_pi * power / order)), float(np.sin(two_pi * power / order))
    return (re * cos - im * sin, re * sin + im * cos)


def short_transform(values, sign):
    order = len(values)
    if order == 1:
        return values
    even = short_transform(values[0::2], sign)
    odd = short_transform(values[1::2], sign)
    turned = [times_root(odd[i], sign * i, order) for i in range(order // 2)]
    return [(even[i][0] + turned[i][0], even[i][1] + turned[i][1]) for i in range(order // 2)] + [
        (even[i][0] - turned[i][0], even[i][1] - turned[i][1]) for i in range(order // 2)
    ]


def conv_kernel(
    values_ref, filter_ref, tables_hbm, twist_hbm, out_ref,
    tables_ref, twist_ref, got_values, got_filter, wave_high, wave_low, signal, result,
    own_sem, send_sem, recv_sem, pass_send, pass_recv,
):
    device = lax.axis_index("ctx")
    group = lax.axis_index("groups")
    count = len(MASKS)
    tokens = values_ref.shape[0]
    block = values_ref.shape[1] // count
    peers = [flip_bits(device, mask) for mask in range(count)]
    barrier = pltpu.get_barrier_semaphore()
    for mask in range(1, count):
        pl.semaphore_signal(
            barrier, inc=1, device_id={"ctx": peers[mask]}, device_id_type=pl.DeviceIdType.MESH
        )
    pl.semaphore_signal(
        barrier, inc=1, device_id={"groups": 1 - group}, device_id_type=pl.DeviceIdType.MESH
    )

    def lanes(index):
        return pl.ds(pl.multiple_of(index * block, block), block)

    def to_peer(kind, mask, src, dst):
        return pltpu.make_async_remote_copy(
            src_ref=src,
            dst_ref=dst,
            send_sem=send_sem.at[kind, mask],
            recv_sem=recv_sem.at[kind, mask],
            device_id={"ctx": peers[mask]},
            device_id_type=pl.DeviceIdType.MESH,
        )

    own = [
        pltpu.make_async_copy(values_ref.at[:, lanes(device)], got_values.at[device], own_sem.at[0]),
        pltpu.make_async_copy(
            filter_ref.at[:, :, :, lanes(device)], got_filter.at[:, :, device], own_sem.at[1]
        ),
    ]
    own += [
        pltpu.make_async_copy(tables_hbm, tables_ref, own_sem.at[2]),
        pltpu.make_async_copy(twist_hbm, twist_ref, own_sem.at[3]),
    ]
    pl.semaphore_wait(barrier, count)
    issue = (15, 7, 14, 6, 13, 5, 12, 4, 11, 3, 10, 2, 9, 1, 8)
    sent_values, sent_filter, passed = {}, {}, {}
    for mask in issue:
        sent_filter[mask] = to_peer(
            1, mask, filter_ref.at[:, group, :, lanes(peers[mask])], got_filter.at[:, group, device]
        )
        sent_filter[mask].start()
    for mask in issue:
        sent_values[mask] = to_peer(
            0, mask, values_ref.at[:, lanes(peers[mask])], got_values.at[device]
        )
        sent_values[mask].start()
    for copy in own:
        copy.start()
    for mask in issue:
        sent_filter[mask].wait_recv()
        slab = got_filter.at[:, group, peers[mask]]
        passed[mask] = pltpu.make_async_remote_copy(
            src_ref=slab,
            dst_ref=slab,
            send_sem=pass_send.at[mask],
            recv_sem=pass_recv.at[mask],
            device_id={"groups": 1 - group},
            device_id_type=pl.DeviceIdType.MESH,
        )
        passed[mask].start()
    for copy in own:
        copy.wait()
    for mask in issue:
        sent_values[mask].wait_recv()

    def reverse(index):
        return int(reverse_bits(count)[index])

    half = tokens
    tile = 16

    @pl.loop(0, tokens // tile)
    def _(step):
        here = pl.ds(pl.multiple_of(step * tile, tile), tile)
        there = pl.ds(pl.multiple_of(half + step * tile, tile), tile)
        samples = [got_values[source, here, :].astype(jnp.float32) for source in range(count)]
        zero = jnp.zeros_like(samples[0])
        for parity in range(2):
            pairs = [
                times_root((item, None), -source * parity, 2 * count)
                for source, item in enumerate(samples)
            ]
            pairs = [(re, zero if im is None else im) for re, im in pairs]
            waves = short_transform(pairs, -1)
            for place in range(count):
                re, im = waves[reverse(place)]
                column = 2 * place + parity
                cos = twist_ref[here, column : column + 1]
                sin = twist_ref[here, 2 * count + column : 2 * count + column + 1]
                for rows, item in ((here, re * cos - im * sin), (there, re * sin + im * cos)):
                    high = item.astype(jnp.bfloat16)
                    columns = slice(column * block, (column + 1) * block)
                    wave_high[rows, columns] = high
                    wave_low[rows, columns] = (item - high.astype(jnp.float32)).astype(jnp.bfloat16)

    width = 4 * block

    def product(which, columns):
        high, low = wave_high[:, columns], wave_low[:, columns]
        return (
            jnp.dot(tables_ref[which], high, preferred_element_type=jnp.float32)
            + jnp.dot(tables_ref[which], low, preferred_element_type=jnp.float32)
            + jnp.dot(tables_ref[which + 1], high, preferred_element_type=jnp.float32)
        )

    steps = 2 * count * block // width

    @pl.loop(0, steps)
    def _(step):
        columns = pl.ds(pl.multiple_of(step * width, width), width)
        signal[:, columns] = product(0, columns)

    for mask in issue:
        passed[mask].wait_recv()

    @pl.loop(0, count)
    def _(place):
        for parity in range(2):
            columns = pl.ds(pl.multiple_of((2 * place + parity) * block, block), block)
            re, im = signal[0:half, columns], signal[half : 2 * half, columns]
            filter_re = got_filter[0, parity, place].astype(jnp.float32)
            filter_im = got_filter[1, parity, place].astype(jnp.float32)
            for rows, item in (
                (slice(0, half), re * filter_re - im * filter_im),
                (slice(half, 2 * half), re * filter_im + im * filter_re),
            ):
                high = item.astype(jnp.bfloat16)
                wave_high[rows, columns] = high
                wave_low[rows, columns] = (item - high.astype(jnp.float32)).astype(jnp.bfloat16)

    @pl.loop(0, steps)
    def _(step):
        columns = pl.ds(pl.multiple_of(step * width, width), width)
        signal[:, columns] = product(2, columns)

    scale = 1.0 / (2 * count * tokens)

    @pl.loop(0, tokens // tile)
    def _(step):
        here = pl.ds(pl.multiple_of(step * tile, tile), tile)
        there = pl.ds(pl.multiple_of(half + step * tile, tile), tile)
        total = None
        for parity in range(2):
            waves = [None] * count
            for place in range(count):
                column = 2 * place + parity
                columns = slice(column * block, (column + 1) * block)
                re, im = signal[here, columns], signal[there, columns]
                cos = twist_ref[here, column : column + 1]
                sin = twist_ref[here, 2 * count + column : 2 * count + column + 1]
                waves[reverse(place)] = (re * cos + im * sin, im * cos - re * sin)
            pairs = short_transform(waves, 1)
            parts = [times_root(pair, source * parity, 2 * count)[0] for source, pair in enumerate(pairs)]
            total = parts if total is None else [left + right for left, right in zip(total, parts)]
        for source in range(count):
            result[source, here, :] = (total[source] * scale).astype(jnp.bfloat16)

    out_ref[:, lanes(device)] = result[device]
    returned = {}
    for mask in issue:
        returned[mask] = to_peer(2, mask, result.at[peers[mask]], out_ref.at[:, lanes(device)])
        returned[mask].start()
    for mask in issue:
        returned[mask].wait()
        passed[mask].wait_send()
        sent_values[mask].wait_send()
        sent_filter[mask].wait_send()


def run_convolution(value_stream, filter_spectrum):
    tokens, channels = value_stream.shape
    count = len(MASKS)
    block = channels // count
    vmem = pl.BlockSpec(memory_space=pltpu.VMEM)
    bf16 = jnp.bfloat16
    return pl.pallas_call(
        conv_kernel,
        out_shape=jax.ShapeDtypeStruct((tokens, channels), bf16),
        in_specs=[pl.BlockSpec(memory_space=pl.ANY)] * 4,
        out_specs=vmem,
        scratch_shapes=[
            pltpu.VMEM((4, 2 * tokens, 2 * tokens), bf16),
            pltpu.VMEM((tokens, 4 * count), jnp.float32),
            pltpu.VMEM((count, tokens, block), bf16),
            pltpu.VMEM((2, 2, count, tokens, block), bf16),
            pltpu.VMEM((2 * tokens, 2 * channels), bf16),
            pltpu.VMEM((2 * tokens, 2 * channels), bf16),
            pltpu.VMEM((2 * tokens, 2 * channels), jnp.float32),
            pltpu.VMEM((count, tokens, block), bf16),
            pltpu.SemaphoreType.DMA((4,)),
            pltpu.SemaphoreType.DMA((3, count)),
            pltpu.SemaphoreType.DMA((3, count)),
            pltpu.SemaphoreType.DMA((count,)),
            pltpu.SemaphoreType.DMA((count,)),
        ],
        compiler_params=pltpu.CompilerParams(
            collective_id=2, has_side_effects=True, vmem_limit_bytes=61 * 1024 * 1024
        ),
    )(value_stream, filter_spectrum, inner_tables(tokens), twist_table(count, tokens))


def expert_kernel(
    conv_ref, stream_hbm, router_ref, ids_ref, slots_ref, wg_hbm, wu_hbm, wd_hbm, out_ref,
    stream_ref, hyena, send_head, send_tail, recv_head, recv_tail, done_head, done_tail, back_head, back_tail,
    rows, hidden, wg, wu, wd, tail_sum, gates, own_sem, send_sem, recv_sem, weight_sem,
):
    device = lax.axis_index("ctx")
    peers = [flip_bits(device, mask) for mask in MASKS]
    count = len(MASKS)
    channels = conv_ref.shape[1]
    quarter = channels // QUARTERS
    tokens = conv_ref.shape[0]
    slots = count * HEAD
    weights = [
        pltpu.make_async_copy(src, dst, weight_sem.at[i])
        for i, (src, dst) in enumerate(((wg_hbm, wg), (wu_hbm, wu), (wd_hbm, wd)))
    ]
    stream_copy = pltpu.make_async_copy(stream_hbm, stream_ref, weight_sem.at[3])
    stream_copy.start()
    barrier = pltpu.get_barrier_semaphore()
    for slot in range(1, count):
        pl.semaphore_signal(
            barrier, inc=1, device_id={"ctx": peers[slot]}, device_id_type=pl.DeviceIdType.MESH
        )
    for copy in weights:
        copy.start()
    ids = ids_ref[...]
    picks = slots_ref[...]
    position = jnp.zeros_like(ids)
    for slot in range(count):
        position = jnp.where(ids == peers[slot], slot, position)
    head = jnp.where(picks < HEAD, position * HEAD + picks, -1024)
    tail = jnp.where((picks >= HEAD) & (picks < CAP), position * HEAD + picks - HEAD, -1024)
    stream_copy.wait()
    mixed = (stream_ref[...].astype(jnp.float32) * conv_ref[...].astype(jnp.float32)).astype(jnp.bfloat16)
    hyena[...] = mixed
    mixed32 = mixed.astype(jnp.float32)
    mean = jnp.sum(mixed32 * mixed32, axis=1, keepdims=True) / channels
    normed = (mixed32 * lax.rsqrt(mean + 1e-06)).astype(jnp.bfloat16)
    slot_row = lax.broadcasted_iota(jnp.int32, (slots, tokens), 0)

    def hits(targets, shift):
        return [slot_row == targets[pick : pick + 1, :] + shift for pick in range(2)]

    def one_hot(targets, shift):
        first, second = hits(targets, shift)
        return jnp.where(first | second, 1.0, 0.0).astype(jnp.bfloat16)

    send_head[...] = jnp.dot(one_hot(head, 0), normed, preferred_element_type=jnp.float32).astype(jnp.bfloat16)
    packed = jnp.zeros((slots, quarter), jnp.float32)
    for part in range(QUARTERS):
        packed = packed + jnp.dot(
            one_hot(tail, TAIL * part),
            normed[:, part * quarter : (part + 1) * quarter],
            preferred_element_type=jnp.float32,
        )
    send_tail[...] = packed.astype(jnp.bfloat16)
    pl.semaphore_wait(barrier, count - 1)

    def exchange(slot, phase):
        here = pl.ds(slot * HEAD, HEAD)
        if phase == 0:
            pairs = ((send_head, recv_head), (send_tail, recv_tail))
        else:
            pairs = ((done_head, back_head), (done_tail, back_tail))
        copies = []
        for which, (src, dst) in enumerate(pairs):
            if slot == 0:
                copies.append(pltpu.make_async_copy(src.at[here], dst.at[here], own_sem.at[phase, which]))
            else:
                copies.append(
                    pltpu.make_async_remote_copy(
                        src_ref=src.at[here],
                        dst_ref=dst.at[here],
                        send_sem=send_sem.at[phase, which, slot],
                        recv_sem=recv_sem.at[phase, which, slot],
                        device_id={"ctx": peers[slot]},
                        device_id_type=pl.DeviceIdType.MESH,
                    )
                )
        return copies

    half = count // 2
    issue = (7, 3, 6, 2, 5, 1, 4, 0, 15, 11, 14, 10, 13, 9, 12, 8)
    outward = {slot: exchange(slot, 0) for slot in range(count)}
    inward = {slot: exchange(slot, 1) for slot in range(count)}
    for slot in issue:
        for copy in outward[slot]:
            copy.start()
    logits = lax.dot_general(
        router_ref[...], normed, (((1,), (1,)), ((), ())), preferred_element_type=jnp.float32
    )
    expert_row = lax.broadcasted_iota(jnp.int32, logits.shape, 0)
    for pick in range(2):
        chosen = jnp.sum(
            jnp.where(expert_row == ids[pick : pick + 1, :], logits, 0.0), axis=0, keepdims=True
        )
        gates[pick : pick + 1, :] = jax.nn.sigmoid(chosen)
    group_rows = half * HEAD
    tail_rows = half * TAIL
    pick_row = lax.broadcasted_iota(jnp.int32, (tail_rows, group_rows), 0)
    pick_col = lax.broadcasted_iota(jnp.int32, (tail_rows, group_rows), 1)
    pick_base = (pick_row // TAIL) * HEAD + pick_row % TAIL
    hidden_size = wg.shape[1]
    for group in range(2):
        for slot in range(group * half, (group + 1) * half):
            for copy in outward[slot]:
                copy.wait()
        span = pl.ds(group * group_rows, group_rows)
        rows[0:group_rows, :] = recv_head[span, :]
        for part in range(QUARTERS):
            select = jnp.where(pick_col == pick_base + TAIL * part, 1.0, 0.0).astype(jnp.bfloat16)
            rows[group_rows : group_rows + tail_rows, part * quarter : (part + 1) * quarter] = jnp.dot(
                select, recv_tail[span, :], preferred_element_type=jnp.float32
            ).astype(jnp.bfloat16)
        if group == 0:
            weights[0].wait()
            weights[1].wait()

        @pl.loop(0, hidden_size // 256)
        def _(step):
            columns = pl.ds(pl.multiple_of(step * 256, 256), 256)
            gate_part = jnp.dot(rows[...], wg[:, columns], preferred_element_type=jnp.float32)
            up_part = jnp.dot(rows[...], wu[:, columns], preferred_element_type=jnp.float32)
            hidden[:, columns] = (jax.nn.silu(gate_part) * up_part).astype(jnp.bfloat16)

        if group == 0:
            weights[2].wait()
        tail_sum[...] = jnp.zeros_like(tail_sum)

        @pl.loop(0, QUARTERS)
        def _(part):
            columns = pl.ds(pl.multiple_of(part * quarter, 256), quarter)
            value = jnp.dot(hidden[...], wd[:, columns], preferred_element_type=jnp.float32).astype(jnp.bfloat16)
            done_head[span, columns] = value[0:group_rows, :]
            select = jnp.where(pick_col == pick_base + TAIL * part, 1.0, 0.0).astype(jnp.bfloat16)
            tail_sum[...] += lax.dot_general(
                select,
                value[group_rows : group_rows + tail_rows, :],
                (((0,), (0,)), ((), ())),
                preferred_element_type=jnp.float32,
            )

        done_tail[span, :] = tail_sum[...].astype(jnp.bfloat16)
        for slot in issue[group * half : (group + 1) * half]:
            for copy in inward[slot]:
                copy.start()

    def weights_of(targets, shift):
        first, second = hits(targets, shift)
        mix = jnp.where(first, gates[0:1, :], 0.0) + jnp.where(second, gates[1:2, :], 0.0)
        high = mix.astype(jnp.bfloat16)
        return high, (mix - high.astype(jnp.float32)).astype(jnp.bfloat16)

    def weighted(pair, values):
        dims = (((0,), (0,)), ((), ()))
        return sum(
            lax.dot_general(piece, values, dims, preferred_element_type=jnp.float32) for piece in pair
        )

    head_pair = weights_of(head, 0)
    tail_pairs = [weights_of(tail, TAIL * part) for part in range(QUARTERS)]
    for slot in range(count):
        for copy in inward[slot]:
            copy.wait()
    out_ref[...] = (hyena[...].astype(jnp.float32) + weighted(head_pair, back_head[...]) + jnp.concatenate(
        [weighted(pair, back_tail[...]) for pair in tail_pairs], axis=1
    )).astype(jnp.bfloat16)


def run_experts(long_conv, gate_stream, router, w_gate, w_up, w_down, route_ids, route_slots):
    tokens, channels = gate_stream.shape
    hidden_size = w_gate.shape[1]
    count = len(MASKS)
    slots = count * HEAD
    half_rows = slots // 2 + (count // 2) * TAIL
    quarter = channels // QUARTERS
    vmem = pl.BlockSpec(memory_space=pltpu.VMEM)
    hbm = pl.BlockSpec(memory_space=pl.ANY)
    bf16 = jnp.bfloat16
    return pl.pallas_call(
        expert_kernel,
        out_shape=jax.ShapeDtypeStruct((tokens, channels), bf16),
        in_specs=[vmem, hbm, vmem, vmem, vmem] + [hbm] * 3,
        out_specs=vmem,
        scratch_shapes=[pltpu.VMEM((tokens, channels), bf16)] * 2
        + [pltpu.VMEM((slots, channels), bf16), pltpu.VMEM((slots, quarter), bf16)] * 4
        + [
            pltpu.VMEM((half_rows, channels), bf16),
            pltpu.VMEM((half_rows, hidden_size), bf16),
            pltpu.VMEM((channels, hidden_size), bf16),
            pltpu.VMEM((channels, hidden_size), bf16),
            pltpu.VMEM((hidden_size, channels), bf16),
            pltpu.VMEM((slots // 2, quarter), jnp.float32),
            pltpu.VMEM((8, tokens), jnp.float32),
            pltpu.SemaphoreType.DMA((2, 2)),
            pltpu.SemaphoreType.DMA((2, 2, count)),
            pltpu.SemaphoreType.DMA((2, 2, count)),
            pltpu.SemaphoreType.DMA((4,)),
        ],
        compiler_params=pltpu.CompilerParams(
            collective_id=1, has_side_effects=True, vmem_limit_bytes=56 * 1024 * 1024
        ),
    )(long_conv, gate_stream, router.T, route_ids, route_slots, w_gate, w_up, w_down)


def local(
    value_stream, gate_stream, filter_spectrum, router, w_gate, w_up, w_down, route_ids, route_slots
):
    tok_rows, channels = value_stream.shape
    size_ctx = lax.axis_size("ctx")
    block = channels // size_ctx
    expert_count = router.shape[1]
    if (
        size_ctx == expert_count == len(MASKS)
        and lax.axis_size("groups") == 2
        and block == tok_rows == 128
        and w_gate.shape[1] % 256 == 0
    ):
        long_conv = run_convolution(value_stream, filter_spectrum)
        return run_experts(
            long_conv, gate_stream, router, w_gate, w_up, w_down, route_ids, route_slots
        )
    arrived = lax.all_to_all(value_stream, "ctx", split_axis=1, concat_axis=0, tiled=True)
    filter_all = lax.all_to_all(filter_spectrum, "ctx", split_axis=3, concat_axis=2, tiled=True)
    long_conv = convolve(arrived, filter_all, size_ctx, tok_rows, block)
    long_conv = lax.all_to_all(
        long_conv.astype(jnp.bfloat16), "ctx", split_axis=0, concat_axis=1, tiled=True
    )
    long_conv = long_conv.astype(jnp.float32)
    hyena_out = (gate_stream.astype(jnp.float32) * long_conv).astype(jnp.bfloat16)
    hyena32 = hyena_out.astype(jnp.float32)
    inv_rms = lax.rsqrt(jnp.mean(hyena32 * hyena32, axis=1, keepdims=True) + 1e-06)
    normed = (hyena32 * inv_rms).astype(jnp.bfloat16)
    logits = jnp.dot(normed, router, preferred_element_type=jnp.float32)
    owner_split = size_ctx // expert_count
    slot_count = expert_count * CAP
    positions = jnp.arange(slot_count, dtype=jnp.int32)
    expert_range = jnp.arange(expert_count, dtype=jnp.int32)
    combine = jnp.zeros((tok_rows, slot_count), jnp.float32)
    dispatch = jnp.zeros((slot_count, channels), jnp.float32)
    for pick_index in range(route_ids.shape[0]):
        expert_ids = route_ids[pick_index]
        slot_ids = route_slots[pick_index]
        target = jnp.where(slot_ids < CAP, expert_ids * CAP + slot_ids, -1)
        slot_hits = target[:, None] == positions[None, :]
        chosen_logit = jnp.sum(
            jnp.where(expert_ids[:, None] == expert_range[None, :], logits, 0.0), axis=1
        )
        gate_value = jax.nn.sigmoid(chosen_logit)
        combine = combine + slot_hits.astype(jnp.float32) * gate_value[:, None]
        dispatch = dispatch + lax.dot_general(
            slot_hits.astype(jnp.bfloat16),
            normed,
            (((0,), (0,)), ((), ())),
            preferred_element_type=jnp.float32,
        )
    buffer = dispatch.astype(jnp.bfloat16).reshape(expert_count, CAP, channels)
    outgoing = jnp.repeat(buffer, owner_split, axis=0)
    slot_rows = lax.all_to_all(outgoing, "ctx", split_axis=0, concat_axis=0, tiled=True)
    flat_rows = slot_rows.reshape(-1, channels)
    gate_part = jnp.dot(flat_rows, w_gate, preferred_element_type=jnp.float32)
    up_part = jnp.dot(flat_rows, w_up, preferred_element_type=jnp.float32)
    hidden = (jax.nn.silu(gate_part) * up_part).astype(jnp.bfloat16)
    partial_value = jnp.dot(hidden, w_down, preferred_element_type=jnp.float32).astype(jnp.bfloat16)
    returned = lax.all_to_all(
        partial_value.reshape(slot_rows.shape), "ctx", split_axis=0, concat_axis=0, tiled=True
    )
    expert_out = jnp.sum(
        returned.astype(jnp.float32).reshape(expert_count, owner_split, CAP, channels), axis=1
    ).reshape(slot_count, channels)
    contribution = jnp.dot(combine, expert_out, precision=highest)
    return (hyena32 + contribution).astype(jnp.bfloat16)


def solution(mesh):
    in_specs = (
        P(("groups", "ctx"), None),
        P(("groups", "ctx"), None),
        P(None, None, "ctx", None),
        P(),
        P(None, "ctx"),
        P(None, "ctx"),
        P("ctx", None),
        P(None, ("groups", "ctx")),
        P(None, ("groups", "ctx")),
    )
    out_specs = P(("groups", "ctx"), None)
    return jax.shard_map(local, mesh=mesh, in_specs=in_specs, out_specs=out_specs, check_vma=False)
```

```python
import jax
import jax.numpy as jnp
import numpy as np
from jax import lax
from jax.experimental import pallas as pl
from jax.experimental.pallas import tpu as pltpu
from jax.sharding import PartitionSpec as P

CAP = 20


two_pi = 2.0 * np.pi
highest = lax.Precision.HIGHEST


def reverse_bits(length_n):
    bit_count = length_n.bit_length() - 1
    positions = np.arange(length_n)
    reversed_index = np.zeros(length_n, dtype=np.int64)
    for position in range(bit_count):
        reversed_index = reversed_index | (positions >> position & 1) << bit_count - 1 - position
    return reversed_index


def spread_table(size_ctx):
    rho = 2 * reverse_bits(size_ctx)[None, :] + np.arange(2)[:, None]
    angle_rad = -two_pi * (np.outer(rho.reshape(-1), np.arange(size_ctx)) % (2 * size_ctx)) / (2 * size_ctx)
    parts = np.stack([np.cos(angle_rad), np.sin(angle_rad)], axis=1)
    return jnp.asarray(parts, jnp.float32)


def fine_table(size_ctx, tok_rows):
    total = 2 * size_ctx * tok_rows
    rho = (2 * reverse_bits(size_ctx)[None, :] + np.arange(2)[:, None]).reshape(-1)
    k = 2 * size_ctx * reverse_bits(tok_rows)[None, :] + rho[:, None]
    step = (k[:, :, None] * np.arange(tok_rows)[None, None, :]) % total
    angle_rad = -two_pi * step / total
    re, im = np.cos(angle_rad), np.sin(angle_rad)
    table = np.stack([np.stack([re, -im], axis=2), np.stack([im, re], axis=2)], axis=1)
    return jnp.asarray(table.reshape(2 * size_ctx, 2 * tok_rows, 2 * tok_rows), jnp.float32)


def convolve(arrived, filter_all, size_ctx, tok_rows, block):
    rho_count = 2 * size_ctx
    coarse = spread_table(size_ctx)
    fine = fine_table(size_ctx, tok_rows)
    samples = arrived.astype(jnp.float32).reshape(size_ctx, tok_rows * block)
    spread = jnp.dot(coarse.reshape(2 * rho_count, size_ctx), samples, precision=highest)
    spread = spread.reshape(rho_count, 2 * tok_rows, block)
    signal = jnp.einsum("rqt,rtc->rqc", fine, spread, precision=highest)
    signal = signal.reshape(rho_count, 2, tok_rows, block)
    filter32 = filter_all.astype(jnp.float32).reshape(2, rho_count, tok_rows, block)
    real_part = signal[:, 0] * filter32[0] - signal[:, 1] * filter32[1]
    imag_part = signal[:, 0] * filter32[1] + signal[:, 1] * filter32[0]
    signal = jnp.concatenate([real_part, imag_part], axis=1)
    spread = jnp.einsum("rqt,rqc->rtc", fine, signal, precision=highest)
    spread = spread.reshape(2 * rho_count, tok_rows * block)
    folded = jnp.dot(coarse.reshape(2 * rho_count, size_ctx).T, spread, precision=highest)
    return (folded / (rho_count * tok_rows)).reshape(size_ctx * tok_rows, block)


def flip_bits(index, mask):
    result = index
    bit = 1
    while bit <= mask:
        if mask & bit:
            result = result + bit * (1 - 2 * ((index // bit) % 2))
        bit *= 2
    return result


MASKS = (0, 1, 2, 3, 8, 9, 10, 11, 4, 5, 6, 7, 12, 13, 14, 15)
HEAD = 16
TAIL = CAP - HEAD
QUARTERS = HEAD // TAIL


def twist_table(size_ctx, tok_rows):
    rho = (2 * reverse_bits(size_ctx)[:, None] + np.arange(2)[None, :]).reshape(-1)
    angle_rad = -two_pi * np.outer(np.arange(tok_rows), rho) / (2 * size_ctx * tok_rows)
    return jnp.asarray(np.concatenate([np.cos(angle_rad), np.sin(angle_rad)], axis=1), jnp.float32)


def inner_tables(tok_rows):
    angle_rad = -two_pi * (np.outer(reverse_bits(tok_rows), np.arange(tok_rows)) % tok_rows) / tok_rows
    re, im = np.cos(angle_rad), np.sin(angle_rad)
    table = np.block([[re, -im], [im, re]]).astype(np.float32)
    pieces = []
    for matrix in (table, table.T):
        high = matrix.astype(jnp.bfloat16)
        low = (matrix - high.astype(np.float32)).astype(jnp.bfloat16)
        pieces += [high, low]
    return jnp.asarray(np.stack(pieces))


def times_root(pair, power, order):
    power %= order
    re, im = pair
    if power == 0:
        return pair
    if im is None and 4 * power % order:
        cos, sin = float(np.cos(two_pi * power / order)), float(np.sin(two_pi * power / order))
        return (re * cos, re * sin)
    if im is None:
        im = jnp.zeros_like(re)
    if 4 * power == order:
        return (-im, re)
    if 2 * power == order:
        return (-re, -im)
    if 4 * power == 3 * order:
        return (im, -re)
    cos, sin = float(np.cos(two_pi * power / order)), float(np.sin(two_pi * power / order))
    return (re * cos - im * sin, re * sin + im * cos)


def short_transform(values, sign):
    order = len(values)
    if order == 1:
        return values
    even = short_transform(values[0::2], sign)
    odd = short_transform(values[1::2], sign)
    turned = [times_root(odd[i], sign * i, order) for i in range(order // 2)]
    return [(even[i][0] + turned[i][0], even[i][1] + turned[i][1]) for i in range(order // 2)] + [
        (even[i][0] - turned[i][0], even[i][1] - turned[i][1]) for i in range(order // 2)
    ]


def conv_kernel(
    values_ref, filter_ref, tables_hbm, twist_hbm, out_ref,
    tables_ref, twist_ref, got_values, got_filter, wave_high, wave_low, signal, result,
    own_sem, send_sem, recv_sem, pass_send, pass_recv,
):
    device = lax.axis_index("ctx")
    group = lax.axis_index("groups")
    count = len(MASKS)
    tokens = values_ref.shape[0]
    block = values_ref.shape[1] // count
    peers = [flip_bits(device, mask) for mask in range(count)]
    barrier = pltpu.get_barrier_semaphore()
    for mask in range(1, count):
        pl.semaphore_signal(
            barrier, inc=1, device_id={"ctx": peers[mask]}, device_id_type=pl.DeviceIdType.MESH
        )
    pl.semaphore_signal(
        barrier, inc=1, device_id={"groups": 1 - group}, device_id_type=pl.DeviceIdType.MESH
    )

    def lanes(index):
        return pl.ds(pl.multiple_of(index * block, block), block)

    def to_peer(kind, mask, src, dst):
        return pltpu.make_async_remote_copy(
            src_ref=src,
            dst_ref=dst,
            send_sem=send_sem.at[kind, mask],
            recv_sem=recv_sem.at[kind, mask],
            device_id={"ctx": peers[mask]},
            device_id_type=pl.DeviceIdType.MESH,
        )

    own = [
        pltpu.make_async_copy(values_ref.at[:, lanes(device)], got_values.at[device], own_sem.at[0]),
        pltpu.make_async_copy(
            filter_ref.at[:, :, :, lanes(device)], got_filter.at[:, :, device], own_sem.at[1]
        ),
    ]
    own += [
        pltpu.make_async_copy(tables_hbm, tables_ref, own_sem.at[2]),
        pltpu.make_async_copy(twist_hbm, twist_ref, own_sem.at[3]),
    ]
    pl.semaphore_wait(barrier, count)
    issue = (15, 7, 14, 6, 13, 5, 12, 4, 11, 3, 10, 2, 9, 1, 8)
    sent_values, sent_filter, passed = {}, {}, {}
    for mask in issue:
        sent_filter[mask] = to_peer(
            1, mask, filter_ref.at[:, group, :, lanes(peers[mask])], got_filter.at[:, group, device]
        )
        sent_filter[mask].start()
    for mask in issue:
        sent_values[mask] = to_peer(
            0, mask, values_ref.at[:, lanes(peers[mask])], got_values.at[device]
        )
        sent_values[mask].start()
    for copy in own:
        copy.start()
    for mask in issue:
        sent_filter[mask].wait_recv()
        slab = got_filter.at[:, group, peers[mask]]
        passed[mask] = pltpu.make_async_remote_copy(
            src_ref=slab,
            dst_ref=slab,
            send_sem=pass_send.at[mask],
            recv_sem=pass_recv.at[mask],
            device_id={"groups": 1 - group},
            device_id_type=pl.DeviceIdType.MESH,
        )
        passed[mask].start()
    for copy in own:
        copy.wait()
    for mask in issue:
        sent_values[mask].wait_recv()

    def reverse(index):
        return int(reverse_bits(count)[index])

    half = tokens
    tile = 16

    @pl.loop(0, tokens // tile)
    def _(step):
        here = pl.ds(pl.multiple_of(step * tile, tile), tile)
        there = pl.ds(pl.multiple_of(half + step * tile, tile), tile)
        samples = [got_values[source, here, :].astype(jnp.float32) for source in range(count)]
        zero = jnp.zeros_like(samples[0])
        for parity in range(2):
            pairs = [
                times_root((item, None), -source * parity, 2 * count)
                for source, item in enumerate(samples)
            ]
            pairs = [(re, zero if im is None else im) for re, im in pairs]
            waves = short_transform(pairs, -1)
            for place in range(count):
                re, im = waves[reverse(place)]
                column = 2 * place + parity
                cos = twist_ref[here, column : column + 1]
                sin = twist_ref[here, 2 * count + column : 2 * count + column + 1]
                for rows, item in ((here, re * cos - im * sin), (there, re * sin + im * cos)):
                    high = item.astype(jnp.bfloat16)
                    columns = slice(column * block, (column + 1) * block)
                    wave_high[rows, columns] = high
                    wave_low[rows, columns] = (item - high.astype(jnp.float32)).astype(jnp.bfloat16)

    width = 4 * block

    def product(which, columns):
        high, low = wave_high[:, columns], wave_low[:, columns]
        return (
            jnp.dot(tables_ref[which], high, preferred_element_type=jnp.float32)
            + jnp.dot(tables_ref[which], low, preferred_element_type=jnp.float32)
            + jnp.dot(tables_ref[which + 1], high, preferred_element_type=jnp.float32)
        )

    steps = 2 * count * block // width

    @pl.loop(0, steps)
    def _(step):
        columns = pl.ds(pl.multiple_of(step * width, width), width)
        signal[:, columns] = product(0, columns)

    for mask in issue:
        passed[mask].wait_recv()

    @pl.loop(0, count)
    def _(place):
        for parity in range(2):
            columns = pl.ds(pl.multiple_of((2 * place + parity) * block, block), block)
            re, im = signal[0:half, columns], signal[half : 2 * half, columns]
            filter_re = got_filter[0, parity, place].astype(jnp.float32)
            filter_im = got_filter[1, parity, place].astype(jnp.float32)
            for rows, item in (
                (slice(0, half), re * filter_re - im * filter_im),
                (slice(half, 2 * half), re * filter_im + im * filter_re),
            ):
                high = item.astype(jnp.bfloat16)
                wave_high[rows, columns] = high
                wave_low[rows, columns] = (item - high.astype(jnp.float32)).astype(jnp.bfloat16)

    @pl.loop(0, steps)
    def _(step):
        columns = pl.ds(pl.multiple_of(step * width, width), width)
        signal[:, columns] = product(2, columns)

    scale = 1.0 / (2 * count * tokens)

    def finish(step):
        here = pl.ds(pl.multiple_of(step * tile, tile), tile)
        there = pl.ds(pl.multiple_of(half + step * tile, tile), tile)
        total = None
        for parity in range(2):
            waves = [None] * count
            for place in range(count):
                column = 2 * place + parity
                columns = slice(column * block, (column + 1) * block)
                re, im = signal[here, columns], signal[there, columns]
                cos = twist_ref[here, column : column + 1]
                sin = twist_ref[here, 2 * count + column : 2 * count + column + 1]
                waves[reverse(place)] = (re * cos + im * sin, im * cos - re * sin)
            pairs = short_transform(waves, 1)
            parts = [times_root(pair, source * parity, 2 * count)[0] for source, pair in enumerate(pairs)]
            total = parts if total is None else [left + right for left, right in zip(total, parts)]
        for source in range(count):
            result[source, here, :] = (total[source] * scale).astype(jnp.bfloat16)

    returned = []
    for part in range(2):
        pl.loop(part * tokens // tile // 2, (part + 1) * tokens // tile // 2)(finish)
        span = pl.ds(part * tokens // 2, tokens // 2)
        for mask in issue:
            copy = to_peer(
                2 + part, mask, result.at[peers[mask], span], out_ref.at[span, lanes(device)]
            )
            copy.start()
            returned.append(copy)
    out_ref[:, lanes(device)] = result[device]
    for copy in returned:
        copy.wait()
    for mask in issue:
        passed[mask].wait_send()
        sent_values[mask].wait_send()
        sent_filter[mask].wait_send()


def run_convolution(value_stream, filter_spectrum):
    tokens, channels = value_stream.shape
    count = len(MASKS)
    block = channels // count
    vmem = pl.BlockSpec(memory_space=pltpu.VMEM)
    bf16 = jnp.bfloat16
    return pl.pallas_call(
        conv_kernel,
        out_shape=jax.ShapeDtypeStruct((tokens, channels), bf16),
        in_specs=[pl.BlockSpec(memory_space=pl.ANY)] * 4,
        out_specs=vmem,
        scratch_shapes=[
            pltpu.VMEM((4, 2 * tokens, 2 * tokens), bf16),
            pltpu.VMEM((tokens, 4 * count), jnp.float32),
            pltpu.VMEM((count, tokens, block), bf16),
            pltpu.VMEM((2, 2, count, tokens, block), bf16),
            pltpu.VMEM((2 * tokens, 2 * channels), bf16),
            pltpu.VMEM((2 * tokens, 2 * channels), bf16),
            pltpu.VMEM((2 * tokens, 2 * channels), jnp.float32),
            pltpu.VMEM((count, tokens, block), bf16),
            pltpu.SemaphoreType.DMA((4,)),
            pltpu.SemaphoreType.DMA((4, count)),
            pltpu.SemaphoreType.DMA((4, count)),
            pltpu.SemaphoreType.DMA((count,)),
            pltpu.SemaphoreType.DMA((count,)),
        ],
        compiler_params=pltpu.CompilerParams(
            collective_id=2, has_side_effects=True, vmem_limit_bytes=61 * 1024 * 1024
        ),
    )(value_stream, filter_spectrum, inner_tables(tokens), twist_table(count, tokens))


def expert_kernel(
    conv_ref, stream_hbm, router_ref, ids_ref, slots_ref, wg_hbm, wu_hbm, wd_hbm, out_ref,
    stream_ref, hyena, send_head, send_tail, recv_head, recv_tail, done_head, done_tail, back_head, back_tail,
    rows, hidden, wg, wu, wd, tail_sum, gates, own_sem, send_sem, recv_sem, weight_sem,
):
    device = lax.axis_index("ctx")
    peers = [flip_bits(device, mask) for mask in MASKS]
    count = len(MASKS)
    channels = conv_ref.shape[1]
    quarter = channels // QUARTERS
    tokens = conv_ref.shape[0]
    slots = count * HEAD
    weights = [
        pltpu.make_async_copy(src, dst, weight_sem.at[i])
        for i, (src, dst) in enumerate(((wg_hbm, wg), (wu_hbm, wu), (wd_hbm, wd)))
    ]
    stream_copy = pltpu.make_async_copy(stream_hbm, stream_ref, weight_sem.at[3])
    stream_copy.start()
    barrier = pltpu.get_barrier_semaphore()
    for slot in range(1, count):
        pl.semaphore_signal(
            barrier, inc=1, device_id={"ctx": peers[slot]}, device_id_type=pl.DeviceIdType.MESH
        )
    for copy in weights:
        copy.start()
    ids = ids_ref[...]
    picks = slots_ref[...]
    position = jnp.zeros_like(ids)
    for slot in range(count):
        position = jnp.where(ids == peers[slot], slot, position)
    head = jnp.where(picks < HEAD, position * HEAD + picks, -1024)
    tail = jnp.where((picks >= HEAD) & (picks < CAP), position * HEAD + picks - HEAD, -1024)
    stream_copy.wait()
    mixed = (stream_ref[...].astype(jnp.float32) * conv_ref[...].astype(jnp.float32)).astype(jnp.bfloat16)
    hyena[...] = mixed
    mixed32 = mixed.astype(jnp.float32)
    mean = jnp.sum(mixed32 * mixed32, axis=1, keepdims=True) / channels
    normed = (mixed32 * lax.rsqrt(mean + 1e-06)).astype(jnp.bfloat16)
    slot_row = lax.broadcasted_iota(jnp.int32, (slots, tokens), 0)

    def hits(targets, shift):
        return [slot_row == targets[pick : pick + 1, :] + shift for pick in range(2)]

    def one_hot(targets, shift):
        first, second = hits(targets, shift)
        return jnp.where(first | second, 1.0, 0.0).astype(jnp.bfloat16)

    send_head[...] = jnp.dot(one_hot(head, 0), normed, preferred_element_type=jnp.float32).astype(jnp.bfloat16)
    packed = jnp.zeros((slots, quarter), jnp.float32)
    for part in range(QUARTERS):
        packed = packed + jnp.dot(
            one_hot(tail, TAIL * part),
            normed[:, part * quarter : (part + 1) * quarter],
            preferred_element_type=jnp.float32,
        )
    send_tail[...] = packed.astype(jnp.bfloat16)
    pl.semaphore_wait(barrier, count - 1)

    def exchange(slot, phase):
        here = pl.ds(slot * HEAD, HEAD)
        if phase == 0:
            pairs = ((send_head, recv_head), (send_tail, recv_tail))
        else:
            pairs = ((done_head, back_head), (done_tail, back_tail))
        copies = []
        for which, (src, dst) in enumerate(pairs):
            if slot == 0:
                copies.append(pltpu.make_async_copy(src.at[here], dst.at[here], own_sem.at[phase, which]))
            else:
                copies.append(
                    pltpu.make_async_remote_copy(
                        src_ref=src.at[here],
                        dst_ref=dst.at[here],
                        send_sem=send_sem.at[phase, which, slot],
                        recv_sem=recv_sem.at[phase, which, slot],
                        device_id={"ctx": peers[slot]},
                        device_id_type=pl.DeviceIdType.MESH,
                    )
                )
        return copies

    half = count // 2
    issue = (7, 3, 6, 2, 5, 1, 4, 0, 15, 11, 14, 10, 13, 9, 12, 8)
    outward = {slot: exchange(slot, 0) for slot in range(count)}
    inward = {slot: exchange(slot, 1) for slot in range(count)}
    for slot in issue:
        for copy in outward[slot]:
            copy.start()
    logits = lax.dot_general(
        router_ref[...], normed, (((1,), (1,)), ((), ())), preferred_element_type=jnp.float32
    )
    expert_row = lax.broadcasted_iota(jnp.int32, logits.shape, 0)
    for pick in range(2):
        chosen = jnp.sum(
            jnp.where(expert_row == ids[pick : pick + 1, :], logits, 0.0), axis=0, keepdims=True
        )
        gates[pick : pick + 1, :] = jax.nn.sigmoid(chosen)
    group_rows = half * HEAD
    tail_rows = half * TAIL
    pick_row = lax.broadcasted_iota(jnp.int32, (tail_rows, group_rows), 0)
    pick_col = lax.broadcasted_iota(jnp.int32, (tail_rows, group_rows), 1)
    pick_base = (pick_row // TAIL) * HEAD + pick_row % TAIL
    hidden_size = wg.shape[1]
    for group in range(2):
        for slot in range(group * half, (group + 1) * half):
            for copy in outward[slot]:
                copy.wait()
        span = pl.ds(group * group_rows, group_rows)
        rows[0:group_rows, :] = recv_head[span, :]
        for part in range(QUARTERS):
            select = jnp.where(pick_col == pick_base + TAIL * part, 1.0, 0.0).astype(jnp.bfloat16)
            rows[group_rows : group_rows + tail_rows, part * quarter : (part + 1) * quarter] = jnp.dot(
                select, recv_tail[span, :], preferred_element_type=jnp.float32
            ).astype(jnp.bfloat16)
        if group == 0:
            weights[0].wait()
            weights[1].wait()

        @pl.loop(0, hidden_size // 256)
        def _(step):
            columns = pl.ds(pl.multiple_of(step * 256, 256), 256)
            gate_part = jnp.dot(rows[...], wg[:, columns], preferred_element_type=jnp.float32)
            up_part = jnp.dot(rows[...], wu[:, columns], preferred_element_type=jnp.float32)
            hidden[:, columns] = (jax.nn.silu(gate_part) * up_part).astype(jnp.bfloat16)

        if group == 0:
            weights[2].wait()
        tail_sum[...] = jnp.zeros_like(tail_sum)

        @pl.loop(0, QUARTERS)
        def _(part):
            columns = pl.ds(pl.multiple_of(part * quarter, 256), quarter)
            value = jnp.dot(hidden[...], wd[:, columns], preferred_element_type=jnp.float32).astype(jnp.bfloat16)
            done_head[span, columns] = value[0:group_rows, :]
            select = jnp.where(pick_col == pick_base + TAIL * part, 1.0, 0.0).astype(jnp.bfloat16)
            tail_sum[...] += lax.dot_general(
                select,
                value[group_rows : group_rows + tail_rows, :],
                (((0,), (0,)), ((), ())),
                preferred_element_type=jnp.float32,
            )

        done_tail[span, :] = tail_sum[...].astype(jnp.bfloat16)
        for slot in issue[group * half : (group + 1) * half]:
            for copy in inward[slot]:
                copy.start()

    def weights_of(targets, shift):
        first, second = hits(targets, shift)
        mix = jnp.where(first, gates[0:1, :], 0.0) + jnp.where(second, gates[1:2, :], 0.0)
        high = mix.astype(jnp.bfloat16)
        return high, (mix - high.astype(jnp.float32)).astype(jnp.bfloat16)

    def weighted(pair, values):
        dims = (((0,), (0,)), ((), ()))
        return sum(
            lax.dot_general(piece, values, dims, preferred_element_type=jnp.float32) for piece in pair
        )

    head_pair = weights_of(head, 0)
    tail_pairs = [weights_of(tail, TAIL * part) for part in range(QUARTERS)]
    for slot in range(count):
        for copy in inward[slot]:
            copy.wait()
    out_ref[...] = (hyena[...].astype(jnp.float32) + weighted(head_pair, back_head[...]) + jnp.concatenate(
        [weighted(pair, back_tail[...]) for pair in tail_pairs], axis=1
    )).astype(jnp.bfloat16)


def run_experts(long_conv, gate_stream, router, w_gate, w_up, w_down, route_ids, route_slots):
    tokens, channels = gate_stream.shape
    hidden_size = w_gate.shape[1]
    count = len(MASKS)
    slots = count * HEAD
    half_rows = slots // 2 + (count // 2) * TAIL
    quarter = channels // QUARTERS
    vmem = pl.BlockSpec(memory_space=pltpu.VMEM)
    hbm = pl.BlockSpec(memory_space=pl.ANY)
    bf16 = jnp.bfloat16
    return pl.pallas_call(
        expert_kernel,
        out_shape=jax.ShapeDtypeStruct((tokens, channels), bf16),
        in_specs=[vmem, hbm, vmem, vmem, vmem] + [hbm] * 3,
        out_specs=vmem,
        scratch_shapes=[pltpu.VMEM((tokens, channels), bf16)] * 2
        + [pltpu.VMEM((slots, channels), bf16), pltpu.VMEM((slots, quarter), bf16)] * 4
        + [
            pltpu.VMEM((half_rows, channels), bf16),
            pltpu.VMEM((half_rows, hidden_size), bf16),
            pltpu.VMEM((channels, hidden_size), bf16),
            pltpu.VMEM((channels, hidden_size), bf16),
            pltpu.VMEM((hidden_size, channels), bf16),
            pltpu.VMEM((slots // 2, quarter), jnp.float32),
            pltpu.VMEM((8, tokens), jnp.float32),
            pltpu.SemaphoreType.DMA((2, 2)),
            pltpu.SemaphoreType.DMA((2, 2, count)),
            pltpu.SemaphoreType.DMA((2, 2, count)),
            pltpu.SemaphoreType.DMA((4,)),
        ],
        compiler_params=pltpu.CompilerParams(
            collective_id=1, has_side_effects=True, vmem_limit_bytes=56 * 1024 * 1024
        ),
    )(long_conv, gate_stream, router.T, route_ids, route_slots, w_gate, w_up, w_down)


def local(
    value_stream, gate_stream, filter_spectrum, router, w_gate, w_up, w_down, route_ids, route_slots
):
    tok_rows, channels = value_stream.shape
    size_ctx = lax.axis_size("ctx")
    block = channels // size_ctx
    expert_count = router.shape[1]
    if (
        size_ctx == expert_count == len(MASKS)
        and lax.axis_size("groups") == 2
        and block == tok_rows == 128
        and w_gate.shape[1] % 256 == 0
    ):
        long_conv = run_convolution(value_stream, filter_spectrum)
        return run_experts(
            long_conv, gate_stream, router, w_gate, w_up, w_down, route_ids, route_slots
        )
    arrived = lax.all_to_all(value_stream, "ctx", split_axis=1, concat_axis=0, tiled=True)
    filter_all = lax.all_to_all(filter_spectrum, "ctx", split_axis=3, concat_axis=2, tiled=True)
    long_conv = convolve(arrived, filter_all, size_ctx, tok_rows, block)
    long_conv = lax.all_to_all(
        long_conv.astype(jnp.bfloat16), "ctx", split_axis=0, concat_axis=1, tiled=True
    )
    long_conv = long_conv.astype(jnp.float32)
    hyena_out = (gate_stream.astype(jnp.float32) * long_conv).astype(jnp.bfloat16)
    hyena32 = hyena_out.astype(jnp.float32)
    inv_rms = lax.rsqrt(jnp.mean(hyena32 * hyena32, axis=1, keepdims=True) + 1e-06)
    normed = (hyena32 * inv_rms).astype(jnp.bfloat16)
    logits = jnp.dot(normed, router, preferred_element_type=jnp.float32)
    owner_split = size_ctx // expert_count
    slot_count = expert_count * CAP
    positions = jnp.arange(slot_count, dtype=jnp.int32)
    expert_range = jnp.arange(expert_count, dtype=jnp.int32)
    combine = jnp.zeros((tok_rows, slot_count), jnp.float32)
    dispatch = jnp.zeros((slot_count, channels), jnp.float32)
    for pick_index in range(route_ids.shape[0]):
        expert_ids = route_ids[pick_index]
        slot_ids = route_slots[pick_index]
        target = jnp.where(slot_ids < CAP, expert_ids * CAP + slot_ids, -1)
        slot_hits = target[:, None] == positions[None, :]
        chosen_logit = jnp.sum(
            jnp.where(expert_ids[:, None] == expert_range[None, :], logits, 0.0), axis=1
        )
        gate_value = jax.nn.sigmoid(chosen_logit)
        combine = combine + slot_hits.astype(jnp.float32) * gate_value[:, None]
        dispatch = dispatch + lax.dot_general(
            slot_hits.astype(jnp.bfloat16),
            normed,
            (((0,), (0,)), ((), ())),
            preferred_element_type=jnp.float32,
        )
    buffer = dispatch.astype(jnp.bfloat16).reshape(expert_count, CAP, channels)
    outgoing = jnp.repeat(buffer, owner_split, axis=0)
    slot_rows = lax.all_to_all(outgoing, "ctx", split_axis=0, concat_axis=0, tiled=True)
    flat_rows = slot_rows.reshape(-1, channels)
    gate_part = jnp.dot(flat_rows, w_gate, preferred_element_type=jnp.float32)
    up_part = jnp.dot(flat_rows, w_up, preferred_element_type=jnp.float32)
    hidden = (jax.nn.silu(gate_part) * up_part).astype(jnp.bfloat16)
    partial_value = jnp.dot(hidden, w_down, preferred_element_type=jnp.float32).astype(jnp.bfloat16)
    returned = lax.all_to_all(
        partial_value.reshape(slot_rows.shape), "ctx", split_axis=0, concat_axis=0, tiled=True
    )
    expert_out = jnp.sum(
        returned.astype(jnp.float32).reshape(expert_count, owner_split, CAP, channels), axis=1
    ).reshape(slot_count, channels)
    contribution = jnp.dot(combine, expert_out, precision=highest)
    return (hyena32 + contribution).astype(jnp.bfloat16)


def solution(mesh):
    in_specs = (
        P(("groups", "ctx"), None),
        P(("groups", "ctx"), None),
        P(None, None, "ctx", None),
        P(),
        P(None, "ctx"),
        P(None, "ctx"),
        P("ctx", None),
        P(None, ("groups", "ctx")),
        P(None, ("groups", "ctx")),
    )
    out_specs = P(("groups", "ctx"), None)
    return jax.shard_map(local, mesh=mesh, in_specs=in_specs, out_specs=out_specs, check_vma=False)
```
